32 devices in a mesh: fsdp: 2 (over x), ctx: 4 (over z), tp: 4 (over y, core).
Axes of the slice: x: 2, y: 2, z: 4, core: 2. Of those that a mesh axis runs over, the one named last changes fastest.
Arguments:
- frames_in: bfloat16 [4, 12544, 768], P(None, ('fsdp', 'ctx', 'tp')), may hold values from -6 to 6
- out_grad: bfloat16 [4, 12544, 768], P(None, ('fsdp', 'ctx', 'tp')), may hold values from -6 to 6
- w_query: bfloat16 [768, 768], P('fsdp', 'tp'), may hold values from -0.3125 to 0.3125
- w_key: bfloat16 [768, 768], P('fsdp', 'tp'), may hold values from -0.3125 to 0.3125
- w_value: bfloat16 [768, 768], P('fsdp', 'tp'), may hold values from -0.21875 to 0.21875
- w_out: bfloat16 [768, 768], P('tp', 'fsdp'), may hold values from -1.5 to 1.5
- w_up: bfloat16 [768, 3072], P('fsdp', 'tp'), may hold values from -0.21875 to 0.21875
- w_down: bfloat16 [3072, 768], P('tp', 'fsdp'), may hold values from -0.109375 to 0.109375
- norm1_gain: bfloat16 [768], P('fsdp'), may hold values from 0.5 to 1.5
- norm1_bias: bfloat16 [768], P('fsdp'), may hold values from -3 to 3
- norm2_gain: bfloat16 [768], P('fsdp'), may hold values from 0.5 to 1.5
- norm2_bias: bfloat16 [768], P('fsdp'), may hold values from -3 to 3
Outputs:
- block_out: bfloat16 [4, 12544, 768], P(None, ('fsdp', 'ctx', 'tp'))
- input_grad: float32 [4, 12544, 768], P(None, ('fsdp', 'ctx', 'tp'))
- grad_query: float32 [768, 768], P('fsdp', 'tp')
- grad_key: float32 [768, 768], P('fsdp', 'tp')
- grad_value: float32 [768, 768], P('fsdp', 'tp')
- grad_out: float32 [768, 768], P('tp', 'fsdp')
- grad_up: float32 [768, 3072], P('fsdp', 'tp')
- grad_down: float32 [3072, 768], P('tp', 'fsdp')
- grad_norm1_gain: float32 [768], P('fsdp')
- grad_norm1_bias: float32 [768], P('fsdp')
- grad_norm2_gain: float32 [768], P('fsdp')
- grad_norm2_bias: float32 [768], P('fsdp')
The draws below stay inside these ranges and needn't reach their ends.
All inputs are finite; a program needn't handle non-finite values.
Results may differ from the reference program's by a relative error of at most 0.012.
The reference program's roundings to bfloat16 on the way count: a program that leaves them out, or rounds other values in their place, can miss the bound.
Values may be sent and summed in bfloat16 or wider, within the bound.
No kernel may reach another device: no remote copies, remote signals or barrier semaphores. Data moves between devices by JAX's collectives and lax.ppermute only.
A program may use at most 128 MiB of HBM per device.

```python
import math
import jax
import jax.numpy as jnp
from jax import lax

D = 768
HEADS = 12
FF = 3072
PLACES = 196
MB = 4
FR_MB = 8
ROWS_MB = 12544


def raised(array, stream_key, source, target, shards_of, factor):
    owner, partner = [(jnp.arange(array.shape[axis_at]) // (array.shape[axis_at] // shards_of)).reshape([-1 if axis == axis_at else 1 for axis in range(array.ndim)]) for axis_at in (source, target)]
    chosen = jax.random.permutation(stream_key, shards_of)[partner]
    strong = (owner == chosen) | (owner == (partner + shards_of // 2) % shards_of)
    return jnp.where(strong, factor * array, array)


def steps_of(stream_key, extent, split, least, high):
    level = 1.0
    for position, blocks in split:
        steps = jax.random.uniform(jax.random.fold_in(jax.random.fold_in(stream_key, 6), position), (blocks,), jnp.float32, least / len(split), high / len(split))
        level = level * jnp.repeat(jnp.exp(steps), extent[position] // blocks).reshape((-1,) + (1,) * (len(extent) - 1 - position))
    return level


def noise(own_key, extent, scale, bound, shards=(), dtype=jnp.bfloat16):
    entries = scale * jax.random.normal(own_key, extent, jnp.float32)
    if shards:
        entries = entries * steps_of(own_key, extent, shards, -0.22, 0.18)
    return jnp.clip(entries, -bound, bound).astype(dtype)


def gaussian_with(rng, extent, deviation, reach, cuts, heavy, held_as=jnp.bfloat16):
    array = deviation * jax.random.normal(rng, extent, jnp.float32)
    if cuts:
        array = array * steps_of(rng, extent, cuts, -0.22, 0.18)
    return jnp.clip(raised(array, jax.random.fold_in(rng, 3), *heavy), -reach, reach).astype(held_as)


def setup_inputs(seed: int = 0) -> dict:
    keys = jax.random.split(jax.random.key(seed), 13)
    return {
        "frames_in": noise(keys[0], (MB, ROWS_MB, D), 1.0, 6.0, ((1, 32),)),
        "out_grad": gaussian_with(keys[1], (MB, ROWS_MB, D), 1.0, 6.0, ((1, 32),), (1, 2, 32, 2.75)),
        "w_query": noise(keys[2], (D, D), (D // 2) ** -0.5, 0.3125, ((0, 2), (1, 4))),
        "w_key": noise(keys[3], (D, D), (D // 2) ** -0.5, 0.3125, ((0, 2), (1, 4))),
        "w_value": noise(keys[4], (D, D), D ** -0.5, 0.21875, ((0, 2), (1, 4))),
        "w_out": noise(keys[5], (D, D), (max(D * 4 // PLACES, 1)) ** -0.5, 1.5, ((0, 4), (1, 2))),
        "w_up": noise(keys[6], (D, FF), D ** -0.5, 0.21875, ((0, 2), (1, 4))),
        "w_down": noise(keys[7], (FF, D), FF ** -0.5, 0.109375, ((0, 4), (1, 2))),
        "norm1_gain": jnp.clip(1.0 + 0.1 * jax.random.normal(keys[8], (D,), jnp.float32), 0.5, 1.5).astype(jnp.bfloat16),
        "norm1_bias": noise(keys[9], (D,), 0.5, 3.0, ((0, 2),)),
        "norm2_gain": jnp.clip(1.0 + 0.1 * jax.random.normal(keys[10], (D,), jnp.float32), 0.5, 1.5).astype(jnp.bfloat16),
        "norm2_bias": noise(keys[11], (D,), 0.5, 3.0, ((0, 2),)),
    }


@jax.custom_vjp
def low(v):
    return lax.optimization_barrier(v.astype(jnp.bfloat16)).astype(jnp.float32)

@jax.custom_vjp
def low_back(v):
    return v

def low_keep(v):
    return (low(v), None)

def low_pass(kept, grad):
    return (grad,)

def back_keep(v):
    return (v, None)

def back_low(kept, grad):
    return (low(grad),)
low.defvjp(low_keep, low_pass)
low_back.defvjp(back_keep, back_low)
EPSILON = 1e-06

def layer_norm(hidden, gain_vector, shift_vec):
    center = hidden - lax.optimization_barrier(jnp.mean(hidden, axis=-1, keepdims=True))
    spread = lax.optimization_barrier(jnp.mean(center * center, axis=-1, keepdims=True))
    return center * lax.rsqrt(spread + EPSILON) * gain_vector + shift_vec

def matmul(left, right):
    return jnp.dot(left, right, precision=lax.Precision.HIGHEST)

def forward(frames, w_query, w_key, w_value, w_out, w_up, w_down, gain_one, shift_one, gain_two, shift_two):
    frame_count, place_count, width = frames.shape
    head_size = width // HEADS
    row_count = frame_count * place_count
    flat_rows = frames.reshape(row_count, width)
    normed = low(layer_norm(flat_rows, gain_one, shift_one))

    def project(weight):
        return low(low_back(matmul(normed, weight))).reshape(frame_count, place_count, HEADS, head_size)
    queries = project(w_query)
    keys_all = project(w_key)
    values_all = project(w_value)
    scores = jnp.einsum('fqhe,fkhe->fhqk', queries, keys_all, precision=lax.Precision.HIGHEST)
    scores = low_back(scores * (1.0 / math.sqrt(head_size)))
    attn_probs = low(jax.nn.softmax(scores, axis=-1))
    mixed_heads = jnp.einsum('fhqk,fkhe->fqhe', attn_probs, values_all, precision=lax.Precision.HIGHEST)
    mixed_heads = low(low_back(mixed_heads)).reshape(row_count, width)
    hidden = flat_rows + low_back(matmul(mixed_heads, w_out))
    second_normalized = low(layer_norm(hidden, gain_two, shift_two))
    inner_act = low_back(matmul(second_normalized, w_up))
    active = low(jax.nn.gelu(inner_act, approximate=False))
    return (hidden + matmul(active, w_down)).reshape(frame_count, place_count, width)

def reference(frames_in, out_grad, w_query, w_key, w_value, w_out, w_up, w_down, norm1_gain, norm1_bias, norm2_gain, norm2_bias):
    frames_all = frames_in.astype(jnp.float32).reshape(-1, FR_MB, PLACES, D)
    grads_all = out_grad.astype(jnp.float32).reshape(-1, FR_MB, PLACES, D)
    params = (w_query.astype(jnp.float32), w_key.astype(jnp.float32), w_value.astype(jnp.float32), w_out.astype(jnp.float32), w_up.astype(jnp.float32), w_down.astype(jnp.float32), norm1_gain.astype(jnp.float32), norm1_bias.astype(jnp.float32), norm2_gain.astype(jnp.float32), norm2_bias.astype(jnp.float32))

    def one_group(totals, group):
        frames_group, grad_group = group
        output, pullback = jax.vjp(forward, frames_group, *params)
        pulled = pullback(grad_group)
        totals = tuple((running + fresh_grad for running, fresh_grad in zip(totals, pulled[1:])))
        return (totals, (output.astype(jnp.bfloat16), pulled[0]))
    start_totals = tuple((jnp.zeros_like(weight_in) for weight_in in params))
    totals, stacked = lax.scan(one_group, start_totals, (frames_all, grads_all))
    outputs, input_grads = stacked
    return (outputs.reshape(MB, ROWS_MB, D), input_grads.reshape(MB, ROWS_MB, D), totals[0], totals[1], totals[2], totals[3], totals[4], totals[5], totals[6], totals[7], totals[8], totals[9])
```

```python
import functools
import math

import jax
import jax.numpy as jnp
from jax import lax
from jax.experimental import pallas as pl
from jax.experimental.pallas import tpu as pltpu
from jax.sharding import PartitionSpec as P

HEADS = 12
PLACES = 196
PADDED = 208

EPSILON = 1e-06
INV_ROOT_TWO = 0.7071067811865476
INV_ROOT_TAU = 0.3989422804014327
LOWEST = -1e30

NORM_ROWS = 32
VMEM_BYTES = 60 * 1024 * 1024


def dot_rows(left, right):
    return lax.dot_general(
        left, right, (((1,), (0,)), ((), ())), preferred_element_type=jnp.float32
    )


def dot_right_t(left, right):
    return lax.dot_general(
        left, right, (((1,), (1,)), ((), ())), preferred_element_type=jnp.float32
    )


def dot_left_t(left, right):
    return lax.dot_general(
        left, right, (((0,), (0,)), ((), ())), preferred_element_type=jnp.float32
    )


def standardize_rows(rows_in):
    center = rows_in - jnp.mean(rows_in, axis=-1, keepdims=True)
    spread = jnp.mean(center * center, axis=-1, keepdims=True)
    reciprocal_spread = lax.rsqrt(spread + EPSILON)
    return (center * reciprocal_spread, reciprocal_spread)


def norm_backward_pass(norm_gradient, gain_vector, centered_rows, reciprocal_spread):
    scaled_result = norm_gradient * gain_vector
    leading_part = jnp.mean(scaled_result, axis=-1, keepdims=True)
    trailing_part = jnp.mean(scaled_result * centered_rows, axis=-1, keepdims=True)
    return reciprocal_spread * (scaled_result - leading_part - centered_rows * trailing_part)


def swap(block, axis, mask):
    count = lax.axis_size(axis)
    return lax.ppermute(block, axis, [(i, i ^ mask) for i in range(count)])


def bits_of(axis):
    return [(axis, 1 << b) for b in reversed(range(lax.axis_size(axis).bit_length() - 1))]


def orders():
    along_f, along_t = bits_of("fsdp"), bits_of("tp")
    first, last = along_t[:-1], along_t[-1:]
    return (along_f + first + last, first + along_f + last)


def piece_masks():
    masks = [0]
    for _, mask in bits_of("tp"):
        masks = [m for m in masks] + [m ^ mask for m in masks]
    return masks


def gather_blocks(block, order):
    held, keys = block[None], [(0, 0)]
    for axis, mask in order:
        held = jnp.concatenate([held, swap(held, axis, mask)], axis=0)
        keys = keys + [
            (f ^ mask, t) if axis == "fsdp" else (f, t ^ mask) for f, t in keys
        ]
    place = {key: n for n, key in enumerate(keys)}
    f_count = lax.axis_size("fsdp")
    mine = lax.axis_index("fsdp")
    full = []
    for t in piece_masks():
        stack = [held[place[(f, t)]] for f in range(f_count)]
        if f_count == 2:
            first = mine == 0
            parts = [
                jnp.where(first, stack[0], stack[1]),
                jnp.where(first, stack[1], stack[0]),
            ]
        else:
            stacked = jnp.stack(stack)
            parts = [
                lax.dynamic_index_in_dim(stacked, mine ^ f, 0, keepdims=False)
                for f in range(f_count)
            ]
        full.append(jnp.concatenate(parts, axis=1))
    return full


def reduce_blocks(held, order, part_axis):
    mine = lax.axis_index("fsdp")
    for axis, mask in reversed(order):
        if axis == "tp":
            half = held.shape[0] // 2
            got = swap(held[half:].astype(jnp.bfloat16), axis, mask)
            held = held[:half] + got.astype(jnp.float32)
        else:
            part = held.shape[part_axis] // 2
            bit = jnp.where((mine & mask) != 0, 1, 0)
            sent = lax.dynamic_slice_in_dim(held, (1 - bit) * part, part, part_axis)
            got = swap(sent.astype(jnp.bfloat16), axis, mask)
            held = lax.dynamic_slice_in_dim(held, bit * part, part, part_axis) + got.astype(
                jnp.float32
            )
    return held[0]


def sum_over_ctx(block):
    count = lax.axis_size("ctx")
    bit = lax.axis_index("ctx") & 1
    rows = block.shape[0] // 2
    sent = lax.dynamic_slice_in_dim(block, (1 - bit) * rows, rows, 0)
    got = swap(sent.astype(jnp.bfloat16), "ctx", 1)
    held = lax.dynamic_slice_in_dim(block, bit * rows, rows, 0) + got.astype(jnp.float32)
    mask = 2
    while mask < count:
        held = held + swap(held.astype(jnp.bfloat16), "ctx", mask).astype(jnp.float32)
        mask *= 2
    other = swap(held.astype(jnp.bfloat16), "ctx", 1).astype(jnp.float32)
    return jnp.where(
        bit == 0,
        jnp.concatenate([held, other], axis=0),
        jnp.concatenate([other, held], axis=0),
    )


def params(flags=None):
    return pltpu.CompilerParams(vmem_limit_bytes=VMEM_BYTES)


def whole(shape):
    return pl.BlockSpec(shape, lambda i: (0,) * len(shape), pipeline_mode=pl.Buffered(1))


def rows_of(count, width):
    return pl.BlockSpec((count, width), lambda i: (i, 0))


def pad_kernel(count, x_ref, g_ref, xo_ref, go_ref):
    for source, target in ((x_ref, xo_ref), (g_ref, go_ref)):
        block = source[0].astype(jnp.float32)
        blank = jnp.zeros((PADDED - PLACES, block.shape[1]), jnp.float32)
        parts = []
        for n in range(count):
            parts += [block[n * PLACES : (n + 1) * PLACES], blank]
        target[...] = jnp.concatenate(parts, axis=0).astype(target.dtype)


def unpad(block):
    count = block.shape[0] // PADDED
    return jnp.concatenate(
        [block[n * PADDED : n * PADDED + PLACES] for n in range(count)], axis=0
    )


def head_masks(head_size):
    lane = lax.broadcasted_iota(jnp.int32, (1, 2 * head_size), 1)
    return lane < head_size


def attend_kernel(
    heads, head_size, x_ref, norm_ref, wqkv_ref, wout_ref,
    xn_ref, qkv_ref, mixed_ref, log_ref, hidden_ref, sn_ref,
):
    width = heads * head_size
    tokens = x_ref[...].astype(jnp.float32)
    hat, _ = standardize_rows(tokens)
    normed = (hat * norm_ref[0:1, :] + norm_ref[1:2, :]).astype(jnp.bfloat16)
    xn_ref[...] = normed
    for part in range(3):
        cut = slice(part * width, (part + 1) * width)
        qkv_ref[:, cut] = dot_right_t(normed, wqkv_ref[cut, :]).astype(jnp.bfloat16)
    low_half = head_masks(head_size)
    scale = 1.0 / math.sqrt(head_size)
    count = tokens.shape[0] // PADDED

    def one_frame(n, carry):
        rows = pl.ds(pl.multiple_of(n * PADDED, 16), PADDED)
        valid = lax.broadcasted_iota(jnp.int32, (1, PADDED), 1) < PLACES
        for pair in range(heads // 2):
            at = pair * 2 * head_size
            q2 = qkv_ref[rows, at : at + 2 * head_size] * jnp.bfloat16(scale)
            k2 = qkv_ref[rows, width + at : width + at + 2 * head_size]
            v2 = qkv_ref[rows, 2 * width + at : 2 * width + at + 2 * head_size]
            outs = []
            for side in range(2):
                keep = low_half if side == 0 else ~low_half
                q1 = jnp.where(keep, q2, jnp.zeros_like(q2))
                scores = jnp.where(valid, dot_right_t(q1, k2), LOWEST)
                top = jnp.max(scores, axis=-1, keepdims=True)
                powers = jnp.exp(scores - top)
                total = jnp.sum(powers, axis=-1, keepdims=True)
                log_ref[rows, 2 * pair + side : 2 * pair + side + 1] = top + jnp.log(total)
                probs = (powers * (1.0 / total)).astype(jnp.bfloat16)
                outs.append(dot_rows(probs, v2))
            mixed_ref[rows, at : at + 2 * head_size] = jnp.where(
                low_half, outs[0], outs[1]
            ).astype(jnp.bfloat16)
        return carry

    lax.fori_loop(0, count, one_frame, 0)
    hidden = tokens + dot_rows(mixed_ref[...], wout_ref[...])
    hidden_ref[...] = hidden
    hat2, _ = standardize_rows(hidden)
    sn_ref[...] = (hat2 * norm_ref[2:3, :] + norm_ref[3:4, :]).astype(jnp.bfloat16)


def forward_kernel(
    tile, sn_ref, cot_ref, snt_ref, cott_ref, wup_ref, wdown_ref,
    y_ref, d_ref, gup_ref, gdown_ref, act_ref, din_ref,
):
    first = pl.program_id(0) == 0
    count = sn_ref.shape[0] // tile

    @pl.when(first)
    def _():
        y_ref[...] = jnp.zeros_like(y_ref)
        d_ref[...] = jnp.zeros_like(d_ref)

    def one_tile(n, carry):
        rows = pl.ds(pl.multiple_of(n * tile, 16), tile)
        wup, wdown = wup_ref[0], wdown_ref[0]
        inner = dot_right_t(sn_ref[rows, :], wup)
        d_active = dot_right_t(cot_ref[rows, :], wdown)
        share = 0.5 * (1.0 + lax.erf(inner * INV_ROOT_TWO))
        active = (inner * share).astype(jnp.bfloat16)
        slope = share + inner * (jnp.exp(-0.5 * inner * inner) * INV_ROOT_TAU)
        d_inner = (d_active * slope).astype(jnp.bfloat16)
        act_ref[rows, :] = active
        din_ref[rows, :] = d_inner
        y_ref[rows, :] += dot_rows(active, wdown)
        d_ref[rows, :] += dot_rows(d_inner, wup)
        return carry

    lax.fori_loop(0, count, one_tile, 0)
    gdown_ref[0] = dot_rows(cott_ref[...], act_ref[...])
    gup_ref[0] = dot_rows(snt_ref[...], din_ref[...])


def backward_kernel(
    heads, head_size, x_ref, cot_ref, y_ref, d_ref, hidden_ref, qkv_ref, log_ref,
    norm_ref, wqkv_ref, wout_ref,
    out_ref, grad_ref, low_ref, dqkv_ref, ngrad_ref, dmix_ref,
):
    width = heads * head_size
    hidden = hidden_ref[...]
    hat2, scale2 = standardize_rows(hidden)
    d_second = d_ref[...]
    d_hidden = cot_ref[...].astype(jnp.float32) + norm_backward_pass(
        d_second, norm_ref[2:3, :], hat2, scale2
    )
    low = d_hidden.astype(jnp.bfloat16)
    low_ref[...] = low
    dmix_ref[...] = dot_right_t(low, wout_ref[...]).astype(jnp.bfloat16)
    second_terms = (
        jnp.sum(d_second * hat2, axis=0, keepdims=True),
        jnp.sum(d_second, axis=0, keepdims=True),
    )
    out_ref[0] = unpad(hidden + y_ref[...]).astype(jnp.bfloat16)
    low_half = head_masks(head_size)
    scale = 1.0 / math.sqrt(head_size)
    count = hidden.shape[0] // PADDED

    def one_frame(n, carry):
        rows = pl.ds(pl.multiple_of(n * PADDED, 16), PADDED)
        valid = lax.broadcasted_iota(jnp.int32, (1, PADDED), 1) < PLACES
        for pair in range(heads // 2):
            at = pair * 2 * head_size
            q2 = qkv_ref[rows, at : at + 2 * head_size]
            qs = q2 * jnp.bfloat16(scale)
            k2 = qkv_ref[rows, width + at : width + at + 2 * head_size]
            v2 = qkv_ref[rows, 2 * width + at : 2 * width + at + 2 * head_size]
            g2 = dmix_ref[rows, at : at + 2 * head_size]
            dq, dk, dv = [], [], []
            for side in range(2):
                keep = low_half if side == 0 else ~low_half
                q1 = jnp.where(keep, qs, jnp.zeros_like(qs))
                g1 = jnp.where(keep, g2, jnp.zeros_like(g2))
                scores = jnp.where(valid, dot_right_t(q1, k2), LOWEST)
                log_total = log_ref[rows, 2 * pair + side : 2 * pair + side + 1]
                probs = jnp.exp(scores - log_total)
                probs_low = probs.astype(jnp.bfloat16)
                d_probs = dot_right_t(g1, v2)
                delta = jnp.sum(d_probs * probs, axis=-1, keepdims=True)
                d_scores = (probs * (d_probs - delta)).astype(jnp.bfloat16)
                dv.append(dot_left_t(probs_low, g2))
                dq.append(dot_rows(d_scores, k2))
                dk.append(dot_left_t(d_scores, q2))
            for part, pieces, factor in ((0, dq, scale), (1, dk, scale), (2, dv, 1.0)):
                dqkv_ref[rows, part * width + at : part * width + at + 2 * head_size] = (
                    jnp.where(low_half, pieces[0], pieces[1]) * factor
                ).astype(jnp.bfloat16)
        return carry

    lax.fori_loop(0, count, one_frame, 0)
    d_first = dot_rows(dqkv_ref[...], wqkv_ref[...])
    hat1, scale1 = standardize_rows(x_ref[...].astype(jnp.float32))
    grad_ref[0] = unpad(
        d_hidden + norm_backward_pass(d_first, norm_ref[0:1, :], hat1, scale1)
    )
    terms = jnp.concatenate(
        (
            jnp.sum(d_first * hat1, axis=0, keepdims=True),
            jnp.sum(d_first, axis=0, keepdims=True),
        )
        + second_terms
        + (jnp.zeros((4, width), jnp.float32),),
        axis=0,
    )

    @pl.when(pl.program_id(0) == 0)
    def _():
        ngrad_ref[...] = terms

    @pl.when(pl.program_id(0) > 0)
    def _():
        ngrad_ref[...] += terms


def on_device(
    frames_in,
    out_grad,
    w_query,
    w_key,
    w_value,
    w_out,
    w_up,
    w_down,
    norm1_gain,
    norm1_bias,
    norm2_gain,
    norm2_bias,
):
    block_count, resident_rows, width = frames_in.shape
    frames_each = resident_rows // PLACES
    block_rows = frames_each * PADDED
    rows = block_count * block_rows
    head_size = width // HEADS
    units = w_query.shape[1]
    hidden_units = w_up.shape[1]
    order_a, order_b = orders()
    pieces = lax.axis_size("tp")
    low, full = jnp.bfloat16, jnp.float32

    norms_here = jnp.stack([norm1_gain, norm1_bias, norm2_gain, norm2_bias])
    norms_here = jnp.pad(norms_here, ((0, NORM_ROWS - 4), (0, 0)))
    qk_all = gather_blocks(jnp.concatenate([w_query.T, w_key.T, norms_here], axis=0), order_a)
    vo_all = gather_blocks(jnp.concatenate([w_value.T, w_out], axis=0), order_b)
    up_all = jnp.stack(gather_blocks(w_up.T, order_a))
    down_all = jnp.stack(gather_blocks(w_down, order_b))

    norms = qk_all[0][2 * units : 2 * units + 8].astype(full)
    qkv_t = jnp.concatenate(
        [p[:units] for p in qk_all]
        + [p[units : 2 * units] for p in qk_all]
        + [p[:units] for p in vo_all],
        axis=0,
    )
    out_rows = jnp.concatenate([p[units:] for p in vo_all], axis=0)

    resident = pl.BlockSpec((1, resident_rows, width), lambda i: (i, 0, 0))
    tokens, cotangent = pl.pallas_call(
        functools.partial(pad_kernel, frames_each),
        name="pad_frames",
        grid=(block_count,),
        in_specs=[resident, resident],
        out_specs=[rows_of(block_rows, width)] * 2,
        out_shape=[jax.ShapeDtypeStruct((rows, width), low)] * 2,
        compiler_params=params(),
    )(frames_in, out_grad)

    normed, qkv, mixed, logs, hidden, second = pl.pallas_call(
        functools.partial(attend_kernel, HEADS, head_size),
        name="attend",
        grid=(block_count,),
        in_specs=[
            rows_of(block_rows, width),
            whole((8, width)),
            whole((3 * width, width)),
            whole((width, width)),
        ],
        out_specs=[
            rows_of(block_rows, width),
            rows_of(block_rows, 3 * width),
            rows_of(block_rows, width),
            rows_of(block_rows, 128),
            rows_of(block_rows, width),
            rows_of(block_rows, width),
        ],
        out_shape=[
            jax.ShapeDtypeStruct((rows, width), low),
            jax.ShapeDtypeStruct((rows, 3 * width), low),
            jax.ShapeDtypeStruct((rows, width), low),
            jax.ShapeDtypeStruct((rows, 128), full),
            jax.ShapeDtypeStruct((rows, width), full),
            jax.ShapeDtypeStruct((rows, width), low),
        ],
        compiler_params=params(),
    )(tokens, norms, qkv_t, out_rows)

    piece = pl.BlockSpec((1, hidden_units, width), lambda i: (i, 0, 0))
    piece_t = pl.BlockSpec((1, width, hidden_units), lambda i: (i, 0, 0))
    down_part, d_second, up_total, down_total = pl.pallas_call(
        functools.partial(forward_kernel, block_rows),
        name="feed_forward",
        grid=(pieces,),
        in_specs=[
            whole((rows, width)),
            whole((rows, width)),
            whole((width, rows)),
            whole((width, rows)),
            piece,
            piece,
        ],
        out_specs=[whole((rows, width)), whole((rows, width)), piece_t, piece_t],
        out_shape=[
            jax.ShapeDtypeStruct((rows, width), full),
            jax.ShapeDtypeStruct((rows, width), full),
            jax.ShapeDtypeStruct((pieces, width, hidden_units), full),
            jax.ShapeDtypeStruct((pieces, width, hidden_units), full),
        ],
        scratch_shapes=[
            pltpu.VMEM((rows, hidden_units), low),
            pltpu.VMEM((rows, hidden_units), low),
        ],
        compiler_params=params(),
    )(second, cotangent, second.T, cotangent.T, up_all, down_all)

    up_sum = reduce_blocks(up_total, order_a, 1)
    down_sum = reduce_blocks(down_total, order_b, 1)
    forward_sum = sum_over_ctx(jnp.concatenate([up_sum, down_sum], axis=0))

    block_out, input_grad, hidden_low, d_qkv, norm_terms = pl.pallas_call(
        functools.partial(backward_kernel, HEADS, head_size),
        name="attend_back",
        grid=(block_count,),
        in_specs=[
            rows_of(block_rows, width),
            rows_of(block_rows, width),
            rows_of(block_rows, width),
            rows_of(block_rows, width),
            rows_of(block_rows, width),
            rows_of(block_rows, 3 * width),
            rows_of(block_rows, 128),
            whole((8, width)),
            whole((3 * width, width)),
            whole((width, width)),
        ],
        out_specs=[
            resident,
            resident,
            rows_of(block_rows, width),
            rows_of(block_rows, 3 * width),
            whole((8, width)),
        ],
        out_shape=[
            jax.ShapeDtypeStruct(frames_in.shape, low),
            jax.ShapeDtypeStruct(frames_in.shape, full),
            jax.ShapeDtypeStruct((rows, width), low),
            jax.ShapeDtypeStruct((rows, 3 * width), low),
            jax.ShapeDtypeStruct((8, width), full),
        ],
        scratch_shapes=[pltpu.VMEM((block_rows, width), low)],
        compiler_params=params(),
    )(tokens, cotangent, down_part, d_second, hidden, qkv, logs, norms, qkv_t, out_rows)

    norm_terms = jnp.pad(norm_terms, ((0, NORM_ROWS - 8), (0, 0)))
    out_total = dot_left_t(mixed, hidden_low)
    qkv_total = dot_left_t(d_qkv, normed)

    def by_piece(*totals):
        return jnp.stack(
            [
                jnp.concatenate(
                    [
                        total[m * units : (m + 1) * units] if total.shape[0] == width else total
                        for total in totals
                    ],
                    axis=0,
                )
                for m in range(pieces)
            ]
        )

    query_total, key_total, value_total = jnp.split(qkv_total, 3, axis=0)
    qk_sum = reduce_blocks(by_piece(query_total, key_total, norm_terms), order_a, 2)
    vo_sum = reduce_blocks(by_piece(value_total, out_total), order_b, 2)
    mixed_sum = sum_over_ctx(jnp.concatenate([qk_sum, vo_sum], axis=0))
    base = 2 * units + NORM_ROWS
    part = w_up.shape[0]
    return (
        block_out,
        input_grad,
        mixed_sum[:units].T,
        mixed_sum[units : 2 * units].T,
        mixed_sum[base : base + units].T,
        mixed_sum[base + units :],
        forward_sum[:part],
        forward_sum[part:].T,
        mixed_sum[2 * units],
        mixed_sum[2 * units + 1],
        mixed_sum[2 * units + 2],
        mixed_sum[2 * units + 3],
    )


def solution(mesh):
    tokens = P(None, ("fsdp", "ctx", "tp"), None)
    weights = (
        P("fsdp", "tp"),
        P("fsdp", "tp"),
        P("fsdp", "tp"),
        P("tp", "fsdp"),
        P("fsdp", "tp"),
        P("tp", "fsdp"),
        P("fsdp"),
        P("fsdp"),
        P("fsdp"),
        P("fsdp"),
    )
    return jax.shard_map(
        on_device,
        mesh=mesh,
        in_specs=(tokens, tokens) + weights,
        out_specs=(tokens, tokens) + weights,
        check_vma=False,
    )
```

```python
import functools
import math

import jax
import jax.numpy as jnp
from jax import lax
from jax.experimental import pallas as pl
from jax.experimental.pallas import tpu as pltpu
from jax.sharding import PartitionSpec as P


HEADS = 12
PLACES = 196
PADDED = 208

EPSILON = 1e-06
INV_ROOT_TWO = 0.7071067811865476
INV_ROOT_TAU = 0.3989422804014327
LOWEST = -1e30

VMEM_BYTES = 60 * 1024 * 1024


def dot_rows(left, right):
    return lax.dot_general(
        left, right, (((1,), (0,)), ((), ())), preferred_element_type=jnp.float32
    )


def dot_right_t(left, right):
    return lax.dot_general(
        left, right, (((1,), (1,)), ((), ())), preferred_element_type=jnp.float32
    )


def dot_left_t(left, right):
    return lax.dot_general(
        left, right, (((0,), (0,)), ((), ())), preferred_element_type=jnp.float32
    )


def standardize_rows(rows_in):
    center = rows_in - jnp.mean(rows_in, axis=-1, keepdims=True)
    spread = jnp.mean(center * center, axis=-1, keepdims=True)
    reciprocal_spread = lax.rsqrt(spread + EPSILON)
    return (center * reciprocal_spread, reciprocal_spread)


def norm_backward_pass(norm_gradient, gain_vector, centered_rows, reciprocal_spread):
    scaled_result = norm_gradient * gain_vector
    leading_part = jnp.mean(scaled_result, axis=-1, keepdims=True)
    trailing_part = jnp.mean(scaled_result * centered_rows, axis=-1, keepdims=True)
    return reciprocal_spread * (scaled_result - leading_part - centered_rows * trailing_part)


def swap(block, axis, mask):
    count = lax.axis_size(axis)
    return lax.ppermute(block, axis, [(i, i ^ mask) for i in range(count)])


def bits_of(axis):
    return [(axis, 1 << b) for b in reversed(range(lax.axis_size(axis).bit_length() - 1))]


def orders():
    along_f, along_t = bits_of("fsdp"), bits_of("tp")
    first, last = along_t[:-1], along_t[-1:]
    return (along_f + first + last, first + along_f + last)


def piece_masks():
    masks = [0]
    for _, mask in bits_of("tp"):
        masks = [m for m in masks] + [m ^ mask for m in masks]
    return masks


class Pack:
    def __init__(self, arrays, pieces, part):
        self.arrays, self.pieces, self.part = arrays, pieces, part

    def copies(self, refs, piece, first, count, target, row):
        mine = lax.axis_index("fsdp")
        made = []
        for array, start, rows, place, mask in self.pieces[piece]:
            low, high = max(first, place), min(first + count, place + rows)
            if low >= high:
                continue
            source = refs[array].at[pl.ds(start + low - place, high - low), :]
            where = pl.ds(row + low - first, high - low)
            if mask is None:
                made.append((source, target.at[where, :]))
            else:
                column = pl.multiple_of((mine ^ mask) * self.part, 128)
                made.append((source, target.at[where, pl.ds(column, self.part)]))
        return made


def start_copies(pairs, sems, at):
    made = [
        pltpu.make_async_copy(source, target, sems.at[at + n])
        for n, (source, target) in enumerate(pairs)
    ]
    for copy in made:
        copy.start()
    return made


def gather_pack(block):
    f_count, t_count = lax.axis_size("fsdp"), lax.axis_size("tp")
    rows, part = block.shape
    if f_count == 2 and t_count == 4 and part % 128 == 0:
        half = rows // 2
        beside_f = swap(block, "fsdp", 1)
        beside_t = swap(block, "tp", 2)
        across = (swap(beside_f[:half], "tp", 2), swap(beside_t[half:], "fsdp", 1))
        here = (block, beside_f, beside_t) + across
        there = tuple(swap(array, "tp", 1) for array in here)
        pieces = []
        for base in (0, len(here)):
            pieces.append([(base, 0, rows, 0, 0), (base + 1, 0, rows, 0, 1)])
            pieces.append(
                [
                    (base + 2, 0, rows, 0, 0),
                    (base + 3, 0, half, 0, 1),
                    (base + 4, 0, half, half, 1),
                ]
            )
        return Pack(here + there, pieces, part)
    held, keys = block[None], [(0, 0)]
    for axis, mask in orders()[0]:
        held = jnp.concatenate([held, swap(held, axis, mask)], axis=0)
        keys = keys + [(f ^ mask, t) if axis == "fsdp" else (f, t ^ mask) for f, t in keys]
    place = {key: n for n, key in enumerate(keys)}
    mine = lax.axis_index("fsdp")
    full = []
    for t in piece_masks():
        stacked = jnp.stack([held[place[(f, t)]] for f in range(f_count)])
        parts = [
            lax.dynamic_index_in_dim(stacked, mine ^ f, 0, keepdims=False)
            for f in range(f_count)
        ]
        full.append(jnp.concatenate(parts, axis=1))
    pieces = [[(p, 0, rows, 0, None)] for p in range(t_count)]
    return Pack(tuple(full), pieces, part)


def gather_columns(block):
    held, masks = [block], [0]
    for axis, mask in bits_of("fsdp"):
        got = swap(jnp.stack(held), axis, mask)
        held = held + [got[n] for n in range(len(held))]
        masks = masks + [m ^ mask for m in masks]
    mine = lax.axis_index("fsdp")
    count = len(held)
    stacked = jnp.stack([held[masks.index(m)] for m in range(count)])
    parts = [
        lax.dynamic_index_in_dim(stacked, mine ^ m, 0, keepdims=False) for m in range(count)
    ]
    return jnp.concatenate(parts, axis=1)


def reduce_step(held, step, piece_axis, part_axis):
    axis, mask = step
    if axis == "tp":
        half = held.shape[piece_axis] // 2
        keep = lax.slice_in_dim(held, 0, half, axis=piece_axis)
        sent = lax.slice_in_dim(held, half, 2 * half, axis=piece_axis)
    else:
        part = held.shape[part_axis] // 2
        bit = jnp.where((lax.axis_index("fsdp") & mask) != 0, 1, 0)
        keep = lax.dynamic_slice_in_dim(held, bit * part, part, part_axis)
        sent = lax.dynamic_slice_in_dim(held, (1 - bit) * part, part, part_axis)
    return keep + swap(sent.astype(jnp.bfloat16), axis, mask).astype(jnp.float32)


def sum_over_ctx(block):
    count = lax.axis_size("ctx")
    bit = lax.axis_index("ctx") & 1
    rows = block.shape[0] // 2
    sent = lax.dynamic_slice_in_dim(block, (1 - bit) * rows, rows, 0)
    got = swap(sent.astype(jnp.bfloat16), "ctx", 1)
    held = lax.dynamic_slice_in_dim(block, bit * rows, rows, 0) + got.astype(jnp.float32)
    mask = 2
    while mask < count:
        got = swap(held.astype(jnp.bfloat16), "ctx", mask)
        held = held + got.astype(jnp.float32)
        mask *= 2
    other = swap(held.astype(jnp.bfloat16), "ctx", 1).astype(jnp.float32)
    return jnp.where(
        bit == 0,
        jnp.concatenate([held, other], axis=0),
        jnp.concatenate([other, held], axis=0),
    )


def sum_in_plane(block):
    for axis in ("tp", "fsdp"):
        for _, mask in reversed(bits_of(axis)):
            block = block + swap(block, axis, mask)
    return block


def params():
    return pltpu.CompilerParams(vmem_limit_bytes=VMEM_BYTES)


def cost(micros):
    return pl.CostEstimate(flops=int(micros * 1.1e9), bytes_accessed=0, transcendentals=0)


def whole(shape):
    return pl.BlockSpec(shape, lambda i: (0,) * len(shape), pipeline_mode=pl.Buffered(1))


def rows_of(count, width, column=0):
    return pl.BlockSpec((count, width), lambda i: (i, column))


def in_place(arrays):
    return [pl.BlockSpec(memory_space=pl.ANY)] * len(arrays)


def pad_kernel(count, x_ref, g_ref, xo_ref, go_ref):
    for source, target in ((x_ref, xo_ref), (g_ref, go_ref)):
        block = source[0].astype(jnp.float32)
        blank = jnp.zeros((PADDED - PLACES, block.shape[1]), jnp.float32)
        parts = []
        for n in range(count):
            parts += [block[n * PLACES : (n + 1) * PLACES], blank]
        target[...] = jnp.concatenate(parts, axis=0).astype(target.dtype)


def pack_near_kernel(q_ref, k_ref, v_ref, o_ref, out_ref):
    units = q_ref.shape[1]
    for n, ref in enumerate((q_ref, k_ref, v_ref)):
        out_ref[n * units : (n + 1) * units, :] = ref[...].T
    out_ref[3 * units :, :] = o_ref[...]


def pack_feed_kernel(up_ref, down_ref, gate_ref, out_ref):
    units = up_ref.shape[1]
    out_ref[:units, :] = up_ref[...].T
    out_ref[units:, :] = down_ref[...]


def unpad(block):
    count = block.shape[0] // PADDED
    return jnp.concatenate(
        [block[n * PADDED : n * PADDED + PLACES] for n in range(count)], axis=0
    )


def low_lanes(head_size):
    lane = lax.broadcasted_iota(jnp.int32, (1, 2 * head_size), 1)
    return lane < head_size


def projection_copies(pack, refs, units, target):
    pieces = len(pack.pieces)
    side = pieces // 2 * units
    made = []
    for p in range(pieces):
        half, place = divmod(p, pieces // 2)
        for kind in range(3):
            row = (half * 3 + kind) * side + place * units
            made += pack.copies(refs, p, kind * units, units, target, row)
    return made


def attend_kernel(heads, head_size, pack, units, *refs):
    count = len(pack.arrays)
    x_ref, norm_ref = refs[:2]
    raw = refs[2 : 2 + count]
    xn_ref, qkv_ref, mixed_ref, log_ref, hidden_ref, sn_ref = refs[2 + count : 8 + count]
    wqkv_ref, wout_ref, sems = refs[8 + count :]
    width = heads * head_size
    side = width // 2

    @pl.when(pl.program_id(0) == 0)
    def _():
        pairs = projection_copies(pack, raw, units, wqkv_ref)
        for p in range(len(pack.pieces)):
            pairs += pack.copies(raw, p, 3 * units, units, wout_ref, p * units)
        for copy in start_copies(pairs, sems, 0):
            copy.wait()

    tokens = x_ref[...].astype(jnp.float32)
    hat, _ = standardize_rows(tokens)
    normed = (hat * norm_ref[0:1, :] + norm_ref[1:2, :]).astype(jnp.bfloat16)
    xn_ref[...] = normed
    for part in range(6):
        cut = slice(part * side, (part + 1) * side)
        qkv_ref[:, cut] = dot_right_t(normed, wqkv_ref[cut, :]).astype(jnp.bfloat16)
    low_half = low_lanes(head_size)
    scale = 1.0 / math.sqrt(head_size)

    def one_frame(n, carry):
        rows = pl.ds(pl.multiple_of(n * PADDED, 16), PADDED)
        valid = lax.broadcasted_iota(jnp.int32, (1, PADDED), 1) < PLACES
        for pair in range(heads // 2):
            half, place = divmod(pair, heads // 4)
            at = 3 * half * side + place * 2 * head_size
            q2 = qkv_ref[rows, at : at + 2 * head_size] * jnp.bfloat16(scale)
            k2 = qkv_ref[rows, side + at : side + at + 2 * head_size]
            v2 = qkv_ref[rows, 2 * side + at : 2 * side + at + 2 * head_size]
            outs = []
            for hand in range(2):
                keep = low_half if hand == 0 else ~low_half
                q1 = jnp.where(keep, q2, jnp.zeros_like(q2))
                scores = jnp.where(valid, dot_right_t(q1, k2), LOWEST)
                top = jnp.max(scores, axis=-1, keepdims=True)
                powers = jnp.exp(scores - top)
                total = jnp.sum(powers, axis=-1, keepdims=True)
                log_ref[rows, 2 * pair + hand : 2 * pair + hand + 1] = top + jnp.log(total)
                probs = (powers * (1.0 / total)).astype(jnp.bfloat16)
                outs.append(dot_rows(probs, v2))
            mixed_ref[rows, 2 * pair * head_size : 2 * (pair + 1) * head_size] = jnp.where(
                low_half, outs[0], outs[1]
            ).astype(jnp.bfloat16)
        return carry

    lax.fori_loop(0, tokens.shape[0] // PADDED, one_frame, 0)
    hidden = tokens + dot_rows(mixed_ref[...], wout_ref[...])
    hidden_ref[...] = hidden
    hat2, _ = standardize_rows(hidden)
    sn_ref[...] = (hat2 * norm_ref[2:3, :] + norm_ref[3:4, :]).astype(jnp.bfloat16)


def forward_kernel(tile, pack, units, *refs):
    count = len(pack.arrays)
    sn_ref, cot_ref, snt_ref, cott_ref, hidden_ref, norm_ref = refs[:6]
    raw = refs[6 : 6 + count]
    out_ref, dh_ref, keep_ref, send_ref, ngrad_ref = refs[6 + count : 11 + count]
    y_ref, act_ref, din_ref, next_ref, wup_ref, wdown_ref, sems = refs[11 + count :]
    step, steps = pl.program_id(0), len(pack.pieces)
    tiles = sn_ref.shape[0] // tile

    def copies_of(p):
        pairs = pack.copies(raw, p, 0, units, next_ref.at[0], 0)
        pairs += pack.copies(raw, p, units, units, next_ref.at[1], 0)
        return [
            pltpu.make_async_copy(source, target, sems.at[n])
            for n, (source, target) in enumerate(pairs)
        ]

    @pl.when(step == 0)
    def _():
        for copy in copies_of(0):
            copy.start()
        y_ref[...] = jnp.zeros_like(y_ref)
        dh_ref[...] = jnp.zeros_like(dh_ref)

    for p in range(steps):

        @pl.when(step == p)
        def _(p=p):
            for copy in copies_of(p):
                copy.wait()
            wup_ref[...] = next_ref[0]
            wdown_ref[...] = next_ref[1]
            if p + 1 < steps:
                for copy in copies_of(p + 1):
                    copy.start()

    def one_tile(n, carry):
        rows = pl.ds(pl.multiple_of(n * tile, 16), tile)
        wup, wdown = wup_ref[...], wdown_ref[...]
        inner = dot_right_t(sn_ref[rows, :], wup)
        d_active = dot_right_t(cot_ref[rows, :], wdown)
        share = 0.5 * (1.0 + lax.erf(inner * INV_ROOT_TWO))
        active = (inner * share).astype(jnp.bfloat16)
        slope = share + inner * (jnp.exp(-0.5 * inner * inner) * INV_ROOT_TAU)
        d_inner = (d_active * slope).astype(jnp.bfloat16)
        act_ref[rows, :] = active
        din_ref[rows, :] = d_inner
        y_ref[rows, :] += dot_rows(active, wdown)
        dh_ref[rows, :] += dot_rows(d_inner, wup)
        return carry

    lax.fori_loop(0, tiles, one_tile, 0)

    @pl.when(step < steps // 2)
    def _():
        keep_ref[0, 0] = dot_rows(snt_ref[...], din_ref[...])
        keep_ref[0, 1] = dot_rows(cott_ref[...], act_ref[...])

    @pl.when(step >= steps // 2)
    def _():
        send_ref[0, 0] = dot_rows(snt_ref[...], din_ref[...]).astype(jnp.bfloat16)
        send_ref[0, 1] = dot_rows(cott_ref[...], act_ref[...]).astype(jnp.bfloat16)

    @pl.when(step == steps - 1)
    def _():
        ngrad_ref[...] = jnp.zeros_like(ngrad_ref)

        def close(n, carry):
            rows = pl.ds(pl.multiple_of(n * tile, 16), tile)
            hidden = hidden_ref[rows, :]
            out_ref[n] = unpad(hidden + y_ref[rows, :]).astype(jnp.bfloat16)
            hat2, scale2 = standardize_rows(hidden)
            d_second = dh_ref[rows, :]
            dh_ref[rows, :] = cot_ref[rows, :].astype(jnp.float32) + norm_backward_pass(
                d_second, norm_ref[2:3, :], hat2, scale2
            )
            ngrad_ref[2:3, :] += jnp.sum(d_second * hat2, axis=0, keepdims=True)
            ngrad_ref[3:4, :] += jnp.sum(d_second, axis=0, keepdims=True)
            return carry

        lax.fori_loop(0, tiles, close, 0)


def backward_kernel(heads, head_size, half, pack, units, *refs):
    count = len(pack.arrays)
    dh_ref, qkv_ref, log_ref = refs[:3]
    raw = refs[3 : 3 + count]
    dqkv_ref, dmix_ref, wout_ref, sems = refs[3 + count :]
    side = heads // 2 * head_size
    scale = 1.0 / math.sqrt(head_size)
    here = len(pack.pieces) // 2

    @pl.when(pl.program_id(0) == 0)
    def _():
        pairs = []
        for n in range(here):
            pairs += pack.copies(raw, half * here + n, 3 * units, units, wout_ref, n * units)
        for copy in start_copies(pairs, sems, 0):
            copy.wait()

    low = dh_ref[...].astype(jnp.bfloat16)
    dmix_ref[...] = dot_right_t(low, wout_ref[...]).astype(jnp.bfloat16)
    low_half = low_lanes(head_size)

    def one_frame(n, carry):
        rows = pl.ds(pl.multiple_of(n * PADDED, 16), PADDED)
        valid = lax.broadcasted_iota(jnp.int32, (1, PADDED), 1) < PLACES
        for pair in range(heads // 4):
            at = pair * 2 * head_size
            q2 = qkv_ref[rows, at : at + 2 * head_size]
            qs = q2 * jnp.bfloat16(scale)
            k2 = qkv_ref[rows, side + at : side + at + 2 * head_size]
            v2 = qkv_ref[rows, 2 * side + at : 2 * side + at + 2 * head_size]
            g2 = dmix_ref[rows, at : at + 2 * head_size]
            dq, dk, dv = [], [], []
            for hand in range(2):
                keep = low_half if hand == 0 else ~low_half
                q1 = jnp.where(keep, qs, jnp.zeros_like(qs))
                g1 = jnp.where(keep, g2, jnp.zeros_like(g2))
                scores = jnp.where(valid, dot_right_t(q1, k2), LOWEST)
                head = half * (heads // 2) + 2 * pair + hand
                probs = jnp.exp(scores - log_ref[rows, head : head + 1])
                probs_low = probs.astype(jnp.bfloat16)
                d_probs = dot_right_t(g1, v2)
                delta = jnp.sum(d_probs * probs, axis=-1, keepdims=True)
                d_scores = (probs * (d_probs - delta)).astype(jnp.bfloat16)
                dv.append(dot_left_t(probs_low, g2))
                dq.append(dot_rows(d_scores, k2))
                dk.append(dot_left_t(d_scores, q2))
            for part, pieces, factor in ((0, dq, scale), (1, dk, scale), (2, dv, 1.0)):
                dqkv_ref[rows, part * side + at : part * side + at + 2 * head_size] = (
                    jnp.where(low_half, pieces[0], pieces[1]) * factor
                ).astype(jnp.bfloat16)
        return carry

    lax.fori_loop(0, low.shape[0] // PADDED, one_frame, 0)


def input_kernel(pack, units, *refs):
    count = len(pack.arrays)
    x_ref, dh_ref, first_ref, last_ref, norm_ref = refs[:5]
    raw = refs[5 : 5 + count]
    grad_ref, ngrad_ref, wqkv_ref, sems = refs[5 + count :]
    side = first_ref.shape[1]

    @pl.when(pl.program_id(0) == 0)
    def _():
        ngrad_ref[...] = jnp.zeros_like(ngrad_ref)
        for copy in start_copies(projection_copies(pack, raw, units, wqkv_ref), sems, 0):
            copy.wait()

    d_first = dot_rows(first_ref[...], wqkv_ref[:side, :])
    d_first += dot_rows(last_ref[...], wqkv_ref[side:, :])
    hat1, scale1 = standardize_rows(x_ref[...].astype(jnp.float32))
    grad_ref[0] = unpad(
        dh_ref[...] + norm_backward_pass(d_first, norm_ref[0:1, :], hat1, scale1)
    )
    ngrad_ref[0:1, :] += jnp.sum(d_first * hat1, axis=0, keepdims=True)
    ngrad_ref[1:2, :] += jnp.sum(d_first, axis=0, keepdims=True)


def on_device(
    frames_in,
    out_grad,
    w_query,
    w_key,
    w_value,
    w_out,
    w_up,
    w_down,
    norm1_gain,
    norm1_bias,
    norm2_gain,
    norm2_bias,
):
    block_count, resident_rows, width = frames_in.shape
    frames_each = resident_rows // PLACES
    block_rows = frames_each * PADDED
    rows = block_count * block_rows
    head_size = width // HEADS
    units = w_query.shape[1]
    part = w_query.shape[0]
    hidden_units = w_up.shape[1]
    order_a, order_b = orders()
    pieces = lax.axis_size("tp")
    low, full = jnp.bfloat16, jnp.float32
    sds = jax.ShapeDtypeStruct

    near = pl.pallas_call(
        pack_near_kernel,
        name="pack_near",
        out_shape=sds((4 * units, part), low),
        compiler_params=params(),
    )(w_query, w_key, w_value, w_out)
    attention = gather_pack(near)
    norms_here = jnp.stack([norm1_gain, norm1_bias, norm2_gain, norm2_bias])
    norms_here = jnp.pad(norms_here, ((0, 4), (0, 0)))
    norms = gather_columns(norms_here).astype(full)
    feed_here = pl.pallas_call(
        pack_feed_kernel,
        name="pack_feed",
        in_specs=[pl.BlockSpec(memory_space=pltpu.VMEM)] * 2 + [pl.BlockSpec(memory_space=pl.ANY)],
        out_shape=sds((2 * hidden_units, part), low),
        compiler_params=params(),
    )(w_up, w_down, attention.arrays[1])
    feed = gather_pack(feed_here)

    resident = pl.BlockSpec((1, resident_rows, width), lambda i: (i, 0, 0))
    tokens, cotangent = pl.pallas_call(
        functools.partial(pad_kernel, frames_each),
        name="pad_frames",
        grid=(block_count,),
        in_specs=[resident, resident],
        out_specs=[rows_of(block_rows, width)] * 2,
        out_shape=[sds((rows, width), low)] * 2,
        compiler_params=params(),
        cost_estimate=cost(5),
    )(frames_in, out_grad)

    normed, qkv, mixed, logs, hidden, second = pl.pallas_call(
        functools.partial(attend_kernel, HEADS, head_size, attention, units),
        name="attend",
        grid=(block_count,),
        in_specs=[rows_of(block_rows, width), whole((8, width))]
        + in_place(attention.arrays),
        out_specs=[
            rows_of(block_rows, width),
            rows_of(block_rows, 3 * width),
            rows_of(block_rows, width),
            rows_of(block_rows, 128),
            rows_of(block_rows, width),
            rows_of(block_rows, width),
        ],
        out_shape=[
            sds((rows, width), low),
            sds((rows, 3 * width), low),
            sds((rows, width), low),
            sds((rows, 128), full),
            sds((rows, width), full),
            sds((rows, width), low),
        ],
        scratch_shapes=[
            pltpu.VMEM((3 * width, width), low),
            pltpu.VMEM((width, width), low),
            pltpu.SemaphoreType.DMA((64,)),
        ],
        compiler_params=params(),
        cost_estimate=cost(30),
    )(tokens, norms, *attention.arrays)

    half = pieces // 2
    keep_block = pl.BlockSpec(
        (1, 2, width, hidden_units), lambda i: (jnp.minimum(i, half - 1), 0, 0, 0)
    )
    send_block = pl.BlockSpec(
        (1, 2, width, hidden_units), lambda i: (jnp.maximum(i - half, 0), 0, 0, 0)
    )
    block_out, d_hidden, feed_keep, feed_send, second_terms = pl.pallas_call(
        functools.partial(forward_kernel, block_rows, feed, hidden_units),
        name="feed_forward",
        grid=(pieces,),
        in_specs=[
            whole((rows, width)),
            whole((rows, width)),
            whole((width, rows)),
            whole((width, rows)),
            whole((rows, width)),
            whole((8, width)),
        ]
        + in_place(feed.arrays),
        out_specs=[
            whole(frames_in.shape),
            whole((rows, width)),
            keep_block,
            send_block,
            whole((8, width)),
        ],
        out_shape=[
            sds(frames_in.shape, low),
            sds((rows, width), full),
            sds((half, 2, width, hidden_units), full),
            sds((half, 2, width, hidden_units), low),
            sds((8, width), full),
        ],
        scratch_shapes=[
            pltpu.VMEM((rows, width), full),
            pltpu.VMEM((rows, hidden_units), low),
            pltpu.VMEM((rows, hidden_units), low),
            pltpu.VMEM((2, hidden_units, width), low),
            pltpu.VMEM((hidden_units, width), low),
            pltpu.VMEM((hidden_units, width), low),
            pltpu.SemaphoreType.DMA((16,)),
        ],
        compiler_params=params(),
        cost_estimate=cost(62),
    )(second, cotangent, second.T, cotangent.T, hidden, norms, *feed.arrays)

    last = order_a[-1]
    steps_a, steps_b = order_a[:-1][::-1], order_b[:-1][::-1]
    feed_got = swap(feed_send, *last)
    out_total = dot_left_t(mixed, d_hidden.astype(low))
    up_held = feed_keep[:, 0] + feed_got[:, 0].astype(full)
    down_held = feed_keep[:, 1] + feed_got[:, 1].astype(full)

    def attention_back(side):
        wide = 3 * width // 2
        return pl.pallas_call(
            functools.partial(backward_kernel, HEADS, head_size, side, attention, units),
            grid=(block_count,),
            in_specs=[
                rows_of(block_rows, width),
                rows_of(block_rows, wide, side),
                rows_of(block_rows, 128),
            ]
            + in_place(attention.arrays),
            out_specs=rows_of(block_rows, wide),
            out_shape=sds((rows, wide), low),
            scratch_shapes=[
                pltpu.VMEM((block_rows, width // 2), low),
                pltpu.VMEM((width // 2, width), low),
                pltpu.SemaphoreType.DMA((16,)),
            ],
            compiler_params=params(),
            cost_estimate=cost(25),
        )(d_hidden, qkv, logs, *attention.arrays)

    side = width // 2
    d_last = attention_back(1)
    last_total = dot_left_t(d_last, normed)
    near_send = jnp.concatenate([last_total, out_total[side:]], axis=0).astype(low)
    near_got = swap(near_send, *last)
    d_lead = attention_back(0)
    for step_a, step_b in zip(steps_a, steps_b):
        up_held = reduce_step(up_held, step_a, 0, 1)
        down_held = reduce_step(down_held, step_b, 0, 1)
    feed_sum = sum_over_ctx(jnp.concatenate([up_held[0], down_held[0]], axis=0))

    lead_total = dot_left_t(d_lead, normed)
    shape = (2, half, units, width)
    a_held = lead_total[: 2 * side] + near_got[: 2 * side].astype(full)
    b_held = jnp.concatenate([lead_total[2 * side :], out_total[:side]], axis=0) + near_got[
        2 * side :
    ].astype(full)
    a_held, b_held = a_held.reshape(shape), b_held.reshape(shape)

    wide = 3 * width // 2
    input_grad, first_terms = pl.pallas_call(
        functools.partial(input_kernel, attention, units),
        name="input_gradient",
        grid=(block_count,),
        in_specs=[
            rows_of(block_rows, width),
            rows_of(block_rows, width),
            rows_of(block_rows, wide),
            rows_of(block_rows, wide),
            whole((8, width)),
        ]
        + in_place(attention.arrays),
        out_specs=[resident, whole((8, width))],
        out_shape=[sds(frames_in.shape, full), sds((8, width), full)],
        scratch_shapes=[
            pltpu.VMEM((3 * width, width), low),
            pltpu.SemaphoreType.DMA((64,)),
        ],
        compiler_params=params(),
        cost_estimate=cost(14),
    )(tokens, d_hidden, d_lead, d_last, norms, *attention.arrays)

    for step_a, step_b in zip(steps_a, steps_b):
        a_held = reduce_step(a_held, step_a, 1, 3)
        b_held = reduce_step(b_held, step_b, 1, 3)
    norm_terms = sum_in_plane(
        jnp.where(
            lax.broadcasted_iota(jnp.int32, first_terms.shape, 0) < 2, first_terms, second_terms
        ),
    )
    norm_terms = lax.dynamic_slice_in_dim(
        norm_terms, lax.axis_index("fsdp") * part, part, 1
    )
    norm_terms = jnp.pad(norm_terms, ((0, 8), (0, 0)))
    near_sum = sum_over_ctx(
        jnp.concatenate(
            [a_held.reshape(-1, part), b_held.reshape(-1, part), norm_terms], axis=0
        ),
    )
    base = 4 * units
    return (
        block_out,
        input_grad,
        near_sum[:units].T,
        near_sum[units : 2 * units].T,
        near_sum[2 * units : 3 * units].T,
        near_sum[3 * units : base],
        feed_sum[:part],
        feed_sum[part:].T,
        near_sum[base],
        near_sum[base + 1],
        near_sum[base + 2],
        near_sum[base + 3],
    )


def solution(mesh):
    tokens = P(None, ("fsdp", "ctx", "tp"), None)
    weights = (
        P("fsdp", "tp"),
        P("fsdp", "tp"),
        P("fsdp", "tp"),
        P("tp", "fsdp"),
        P("fsdp", "tp"),
        P("tp", "fsdp"),
        P("fsdp"),
        P("fsdp"),
        P("fsdp"),
        P("fsdp"),
    )
    return jax.shard_map(
        on_device,
        mesh=mesh,
        in_specs=(tokens, tokens) + weights,
        out_specs=(tokens, tokens) + weights,
        check_vma=False,
    )
```

```python
import functools
import math

import jax
import jax.numpy as jnp
from jax import lax
from jax.experimental import pallas as pl
from jax.experimental.pallas import tpu as pltpu
from jax.sharding import PartitionSpec as P


HEADS = 12
PLACES = 196
PADDED = 208

EPSILON = 1e-06
INV_ROOT_TWO = 0.7071067811865476
INV_ROOT_TAU = 0.3989422804014327
LOWEST = -1e30

VMEM_BYTES = 60 * 1024 * 1024


def dot_rows(left, right):
    return lax.dot_general(
        left, right, (((1,), (0,)), ((), ())), preferred_element_type=jnp.float32
    )


def dot_right_t(left, right):
    return lax.dot_general(
        left, right, (((1,), (1,)), ((), ())), preferred_element_type=jnp.float32
    )


def dot_left_t(left, right):
    return lax.dot_general(
        left, right, (((0,), (0,)), ((), ())), preferred_element_type=jnp.float32
    )


def standardize_rows(rows_in):
    center = rows_in - jnp.mean(rows_in, axis=-1, keepdims=True)
    spread = jnp.mean(center * center, axis=-1, keepdims=True)
    reciprocal_spread = lax.rsqrt(spread + EPSILON)
    return (center * reciprocal_spread, reciprocal_spread)


def norm_backward_pass(norm_gradient, gain_vector, centered_rows, reciprocal_spread):
    scaled_result = norm_gradient * gain_vector
    leading_part = jnp.mean(scaled_result, axis=-1, keepdims=True)
    trailing_part = jnp.mean(scaled_result * centered_rows, axis=-1, keepdims=True)
    return reciprocal_spread * (scaled_result - leading_part - centered_rows * trailing_part)


def swap(block, axis, mask):
    count = lax.axis_size(axis)
    return lax.ppermute(block, axis, [(i, i ^ mask) for i in range(count)])


def bits_of(axis):
    return [(axis, 1 << b) for b in reversed(range(lax.axis_size(axis).bit_length() - 1))]


def orders():
    along_f, along_t = bits_of("fsdp"), bits_of("tp")
    first, last = along_t[:-1], along_t[-1:]
    return (along_f + first + last, first + along_f + last)


def piece_masks():
    masks = [0]
    for _, mask in bits_of("tp"):
        masks = [m for m in masks] + [m ^ mask for m in masks]
    return masks


class Pack:
    def __init__(self, arrays, pieces, part):
        self.arrays, self.pieces, self.part = arrays, pieces, part

    def copies(self, refs, piece, first, count, target, row):
        mine = lax.axis_index("fsdp")
        made = []
        for array, start, rows, place, mask in self.pieces[piece]:
            low, high = max(first, place), min(first + count, place + rows)
            if low >= high:
                continue
            source = refs[array].at[pl.ds(start + low - place, high - low), :]
            where = pl.ds(row + low - first, high - low)
            if mask is None:
                made.append((source, target.at[where, :]))
            else:
                column = pl.multiple_of((mine ^ mask) * self.part, 128)
                made.append((source, target.at[where, pl.ds(column, self.part)]))
        return made


def copies_on(pairs, sems, at=0):
    return [
        pltpu.make_async_copy(source, target, sems.at[at + n])
        for n, (source, target) in enumerate(pairs)
    ]


def start_all(copies):
    for copy in copies:
        copy.start()


def wait_all(copies):
    for copy in copies:
        copy.wait()


def gather_pack(block):
    f_count, t_count = lax.axis_size("fsdp"), lax.axis_size("tp")
    rows, part = block.shape
    if f_count == 2 and t_count == 4 and part % 128 == 0:
        half = rows // 2
        beside_f = swap(block, "fsdp", 1)
        beside_t = swap(block, "tp", 2)
        across = (swap(beside_f[:half], "tp", 2), swap(beside_t[half:], "fsdp", 1))
        here = (block, beside_f, beside_t) + across
        there = tuple(swap(array, "tp", 1) for array in here)
        pieces = []
        for base in (0, len(here)):
            pieces.append([(base, 0, rows, 0, 0), (base + 1, 0, rows, 0, 1)])
            pieces.append(
                [
                    (base + 2, 0, rows, 0, 0),
                    (base + 3, 0, half, 0, 1),
                    (base + 4, 0, half, half, 1),
                ]
            )
        return Pack(here + there, pieces, part)
    held, keys = block[None], [(0, 0)]
    for axis, mask in orders()[0]:
        held = jnp.concatenate([held, swap(held, axis, mask)], axis=0)
        keys = keys + [(f ^ mask, t) if axis == "fsdp" else (f, t ^ mask) for f, t in keys]
    place = {key: n for n, key in enumerate(keys)}
    mine = lax.axis_index("fsdp")
    full = []
    for t in piece_masks():
        stacked = jnp.stack([held[place[(f, t)]] for f in range(f_count)])
        parts = [
            lax.dynamic_index_in_dim(stacked, mine ^ f, 0, keepdims=False)
            for f in range(f_count)
        ]
        full.append(jnp.concatenate(parts, axis=1))
    pieces = [[(p, 0, rows, 0, None)] for p in range(t_count)]
    return Pack(tuple(full), pieces, part)


def gather_columns(vectors):
    held, masks = [jnp.concatenate(vectors)], [0]
    for axis, mask in bits_of("fsdp"):
        got = swap(jnp.concatenate(held), axis, mask)
        held = held + jnp.split(got, len(held))
        masks = masks + [m ^ mask for m in masks]
    mine = lax.axis_index("fsdp")
    count = len(held)
    parts = [held[masks.index(m)].reshape(len(vectors), -1) for m in range(count)]
    if count == 2:
        first = mine == 0
        parts = [jnp.where(first, parts[0], parts[1]), jnp.where(first, parts[1], parts[0])]
    else:
        stacked = jnp.stack(parts)
        parts = [
            lax.dynamic_index_in_dim(stacked, mine ^ m, 0, keepdims=False) for m in range(count)
        ]
    return jnp.pad(jnp.concatenate(parts, axis=1), ((0, 8 - len(vectors)), (0, 0)))


def reduce_step(held, step, piece_axis, part_axis):
    axis, mask = step
    if axis == "tp":
        half = held.shape[piece_axis] // 2
        keep = lax.slice_in_dim(held, 0, half, axis=piece_axis)
        sent = lax.slice_in_dim(held, half, 2 * half, axis=piece_axis)
    else:
        part = held.shape[part_axis] // 2
        bit = jnp.where((lax.axis_index("fsdp") & mask) != 0, 1, 0)
        keep = lax.dynamic_slice_in_dim(held, bit * part, part, part_axis)
        sent = lax.dynamic_slice_in_dim(held, (1 - bit) * part, part, part_axis)
    return keep + swap(sent.astype(jnp.bfloat16), axis, mask).astype(jnp.float32)


def sum_over_ctx(block):
    count = lax.axis_size("ctx")
    bit = lax.axis_index("ctx") & 1
    rows = block.shape[0] // 2
    sent = lax.dynamic_slice_in_dim(block, (1 - bit) * rows, rows, 0)
    got = swap(sent.astype(jnp.bfloat16), "ctx", 1)
    held = lax.dynamic_slice_in_dim(block, bit * rows, rows, 0) + got.astype(jnp.float32)
    mask = 2
    while mask < count:
        got = swap(held.astype(jnp.bfloat16), "ctx", mask)
        held = held + got.astype(jnp.float32)
        mask *= 2
    other = swap(held.astype(jnp.bfloat16), "ctx", 1).astype(jnp.float32)
    return jnp.where(
        bit == 0,
        jnp.concatenate([held, other], axis=0),
        jnp.concatenate([other, held], axis=0),
    )


def sum_over(block, axes):
    for axis in axes:
        for _, mask in reversed(bits_of(axis)):
            block = block + swap(block, axis, mask)
    return block


def params():
    return pltpu.CompilerParams(vmem_limit_bytes=VMEM_BYTES)


def cost(micros):
    return pl.CostEstimate(flops=int(micros * 1.1e9), bytes_accessed=0, transcendentals=0)


def whole(shape):
    return pl.BlockSpec(shape, lambda i: (0,) * len(shape), pipeline_mode=pl.Buffered(1))


def rows_of(count, width, column=0):
    return pl.BlockSpec((count, width), lambda i: (i, column))


def in_place(arrays):
    return [pl.BlockSpec(memory_space=pl.ANY)] * len(arrays)


def prepare_kernel(count, x_ref, g_ref, norm_ref, xo_ref, go_ref, got_ref, xn_ref):
    blank = jnp.zeros((PADDED - PLACES, x_ref.shape[2]), jnp.float32)
    block_rows = count * PADDED

    def padded(block):
        parts = []
        for n in range(count):
            parts += [block[n * PLACES : (n + 1) * PLACES], blank]
        return jnp.concatenate(parts, axis=0)

    def one_block(n, carry):
        rows = pl.ds(pl.multiple_of(n * block_rows, 16), block_rows)
        tokens = padded(x_ref[n].astype(jnp.float32))
        xo_ref[rows, :] = tokens.astype(jnp.bfloat16)
        hat, _ = standardize_rows(tokens)
        xn_ref[rows, :] = (hat * norm_ref[0:1, :] + norm_ref[1:2, :]).astype(jnp.bfloat16)
        go_ref[rows, :] = padded(g_ref[n].astype(jnp.float32)).astype(jnp.bfloat16)
        return carry

    lax.fori_loop(0, x_ref.shape[0], one_block, 0)
    turn(go_ref, got_ref)


def turn(source, target):
    for start in range(0, source.shape[0], 128):
        target[:, start : start + 128] = source[start : start + 128, :].T


def turn_kernel(source_ref, target_ref):
    turn(source_ref, target_ref)


def pack_near_kernel(q_ref, k_ref, v_ref, o_ref, out_ref):
    units = q_ref.shape[0]
    for n, ref in enumerate((q_ref, k_ref, v_ref, o_ref)):
        out_ref[n * units : (n + 1) * units, :] = ref[...]


def pack_feed_kernel(up_ref, down_ref, gate_ref, out_ref):
    units = up_ref.shape[1]
    out_ref[:units, :] = up_ref[...].T
    out_ref[units:, :] = down_ref[...]


def unpad(block):
    count = block.shape[0] // PADDED
    return jnp.concatenate(
        [block[n * PADDED : n * PADDED + PLACES] for n in range(count)], axis=0
    )


def low_lanes(head_size):
    lane = lax.broadcasted_iota(jnp.int32, (1, 2 * head_size), 1)
    return lane < head_size


def staggered(count, begin, middle, end):
    begun, half_done = {0: begin(0)}, {}
    for n in range(count + 1):
        if n + 1 < count:
            begun[n + 1] = begin(n + 1)
        if n < count:
            half_done[n] = middle(n, begun.pop(n))
        if n > 0:
            end(n - 1, half_done.pop(n - 1))


def both_hands(block, low_half):
    blank = jnp.zeros_like(block)
    return jnp.concatenate(
        [jnp.where(low_half, block, blank), jnp.where(low_half, blank, block)], axis=0
    )


def projection_copies(pack, refs, units, target, groups):
    pieces = len(pack.pieces)
    side = pieces // 2 * units
    made = []
    for group in groups:
        half, kind = divmod(group, 3)
        for n in range(pieces // 2):
            row = group * side + n * units
            made += pack.copies(
                refs, half * pieces // 2 + n, kind * units, units, target, row
            )
    return made


def attend_kernel(heads, head_size, pack, units, *refs):
    count = len(pack.arrays)
    x_ref, xn_ref, norm_ref = refs[:3]
    raw = refs[3 : 3 + count]
    qkv_ref, mixed_ref, log_ref, hidden_ref, sn_ref = refs[3 + count : 8 + count]
    wqkv_ref, wout_ref, sems = refs[8 + count :]
    width = heads * head_size
    side = width // 2

    first = pl.program_id(0) == 0
    batches, used = [], 0
    for n in range(3):
        pairs = projection_copies(pack, raw, units, wqkv_ref, (2 * n, 2 * n + 1))
        batches.append(copies_on(pairs, sems, used))
        used += len(pairs)
    pairs = []
    for p in range(len(pack.pieces)):
        pairs += pack.copies(raw, p, 3 * units, units, wout_ref, p * units)
    batches.append(copies_on(pairs, sems, used))

    @pl.when(first)
    def _():
        for batch in batches:
            start_all(batch)

    normed = xn_ref[...]

    def project(n, carry):
        for k in range(3):

            @pl.when(first & (n == k))
            def _(k=k):
                wait_all(batches[k])

        cut = pl.ds(pl.multiple_of(n * width, 128), width)
        qkv_ref[:, cut] = dot_right_t(normed, wqkv_ref[cut, :]).astype(jnp.bfloat16)
        return carry

    lax.fori_loop(0, 3, project, 0)
    low_half = low_lanes(head_size)
    scale = 1.0 / math.sqrt(head_size)

    def one_frame(n, carry):
        rows = pl.ds(pl.multiple_of(n * PADDED, 16), PADDED)
        valid = lax.broadcasted_iota(jnp.int32, (1, PADDED), 1) < PLACES

        def begin(pair):
            half, place = divmod(pair, heads // 4)
            at = 3 * half * side + place * 2 * head_size
            q2 = qkv_ref[rows, at : at + 2 * head_size] * jnp.bfloat16(scale)
            k2 = qkv_ref[rows, side + at : side + at + 2 * head_size]
            return dot_right_t(both_hands(q2, low_half), k2)

        def middle(pair, scores):
            scores = jnp.where(valid, scores, LOWEST)
            top = jnp.max(scores, axis=-1, keepdims=True)
            powers = jnp.exp(scores - top)
            total = jnp.sum(powers, axis=-1, keepdims=True)
            logs = top + jnp.log(total)
            log_ref[rows, 2 * pair : 2 * pair + 1] = logs[:PADDED]
            log_ref[rows, 2 * pair + 1 : 2 * pair + 2] = logs[PADDED:]
            return (powers * (1.0 / total)).astype(jnp.bfloat16)

        def end(pair, probs):
            half, place = divmod(pair, heads // 4)
            at = (3 * half + 2) * side + place * 2 * head_size
            outs = dot_rows(probs, qkv_ref[rows, at : at + 2 * head_size])
            mixed_ref[rows, 2 * pair * head_size : 2 * (pair + 1) * head_size] = jnp.where(
                low_half, outs[:PADDED], outs[PADDED:]
            ).astype(jnp.bfloat16)

        staggered(heads // 2, begin, middle, end)
        return carry

    lax.fori_loop(0, normed.shape[0] // PADDED, one_frame, 0)

    @pl.when(first)
    def _():
        wait_all(batches[3])

    hidden = x_ref[...].astype(jnp.float32) + dot_rows(mixed_ref[...], wout_ref[...])
    hidden_ref[...] = hidden
    hat2, _ = standardize_rows(hidden)
    sn_ref[...] = (hat2 * norm_ref[2:3, :] + norm_ref[3:4, :]).astype(jnp.bfloat16)


def forward_kernel(tile, pack, units, *refs):
    count = len(pack.arrays)
    arrays, norm_ref = refs[:5], refs[5]
    raw = refs[6 : 6 + count]
    out_any, low_any, keep_any, send_ref, ngrad_ref = refs[6 + count : 11 + count]
    held = refs[11 + count : 16 + count]
    sn_ref, cot_ref, snt_ref, cott_ref, hidden_ref = held
    (
        y_ref, dh_ref, act_ref, din_ref, next_ref, wup_ref, wdown_ref, wupt_ref, wdownt_ref,
        keep_ref, out_ref, low_ref, sems, held_sems, keep_sems, out_sems, low_sems,
    ) = refs[16 + count :]
    step, steps = pl.program_id(0), len(pack.pieces)
    tiles = sn_ref.shape[0] // tile
    chunk = sn_ref.shape[1] // tiles
    wide = 2 * tile
    order = [(n + steps // 2) % steps for n in range(steps)]
    late = copies_on(zip(arrays, held), held_sems)

    def copies_of(n):
        pairs = pack.copies(raw, order[n], 0, units, next_ref.at[0], 0)
        pairs += pack.copies(raw, order[n], units, units, next_ref.at[1], 0)
        return copies_on(pairs, sems)

    @pl.when(step == 0)
    def _():
        start_all(copies_of(0) + late)
        y_ref[...] = jnp.zeros_like(y_ref)
        dh_ref[...] = jnp.zeros_like(dh_ref)

    def settle(n, size):
        rows = pl.ds(pl.multiple_of(n * size, 128), size)
        for place, plain, turned in ((0, wup_ref, wupt_ref), (1, wdown_ref, wdownt_ref)):
            block = next_ref[place, rows, :]
            plain[rows, :] = block
            turned[:, rows] = block.T

    def settle_all():
        def one(n, carry):
            settle(n, units // 2)
            return carry

        lax.fori_loop(0, 2, one, 0)

    @pl.when(step == 0)
    def _():
        wait_all(copies_of(0))
        settle_all()
        start_all(copies_of(1))
        wait_all(late[:2])

    def one_tile(n, carry):
        rows = pl.ds(pl.multiple_of(n * wide, 16), wide)
        inner = dot_rows(sn_ref[rows, :], wupt_ref[...])
        d_active = dot_rows(cot_ref[rows, :], wdownt_ref[...])
        share = 0.5 * (1.0 + lax.erf(inner * INV_ROOT_TWO))
        active = (inner * share).astype(jnp.bfloat16)
        slope = share + inner * (jnp.exp(-0.5 * inner * inner) * INV_ROOT_TAU)
        d_inner = (d_active * slope).astype(jnp.bfloat16)
        act_ref[rows, :] = active
        din_ref[rows, :] = d_inner
        y_ref[rows, :] += dot_rows(active, wdown_ref[...])
        dh_ref[rows, :] += dot_rows(d_inner, wup_ref[...])
        return carry

    lax.fori_loop(0, tiles // 2, one_tile, 0)

    @pl.when(step == 0)
    def _():
        wait_all(late[2:4])

    def weight_gradients(rows):
        keep_ref[0, rows, :] = dot_rows(snt_ref[rows, :], din_ref[...])
        keep_ref[1, rows, :] = dot_rows(cott_ref[rows, :], act_ref[...])

    def whole_keep(p):
        return pltpu.make_async_copy(
            keep_ref, keep_any.at[p - steps // 2], keep_sems.at[0]
        )

    for p in range(steps // 2 + 1, steps):

        @pl.when(step == p)
        def _(p=p):
            whole_keep(p - 1).wait()

    for p in range(1, steps):

        @pl.when(step == p - 1)
        def _(p=p):
            wait_all(copies_of(p))

    @pl.when(step < steps - 1)
    def _():
        weight_gradients(slice(None))
        for n in range(2):
            settle(n, units // 2)

    @pl.when(step < steps // 2)
    def _():
        send_ref[0] = keep_ref[...].astype(jnp.bfloat16)

    for p in range(steps // 2, steps - 1):

        @pl.when(step == p)
        def _(p=p):
            whole_keep(p).start()

    for p in range(2, steps):

        @pl.when(step == p - 2)
        def _(p=p):
            start_all(copies_of(p))

    @pl.when(step == steps - 1)
    def _():
        ngrad_ref[...] = jnp.zeros_like(ngrad_ref)
        wait_all(late[4:])

        def results(n):
            rows = pl.ds(pl.multiple_of(n * tile, 16), tile)
            part = pl.ds(pl.multiple_of(n * chunk, 16), chunk)
            return [
                pltpu.make_async_copy(out_ref.at[n], out_any.at[n], out_sems.at[n]),
                pltpu.make_async_copy(low_ref.at[rows, :], low_any.at[rows, :], low_sems.at[n]),
                pltpu.make_async_copy(
                    keep_ref.at[:, part, :],
                    keep_any.at[steps // 2 - 1, :, part, :],
                    keep_sems.at[1 + n],
                ),
            ]

        def close(n, carry):
            weight_gradients(pl.ds(pl.multiple_of(n * chunk, 16), chunk))
            rows = pl.ds(pl.multiple_of(n * tile, 16), tile)
            hidden = hidden_ref[rows, :]
            out_ref[n] = unpad(hidden + y_ref[rows, :]).astype(jnp.bfloat16)
            hat2, scale2 = standardize_rows(hidden)
            d_second = dh_ref[rows, :]
            d_hidden = cot_ref[rows, :].astype(jnp.float32) + norm_backward_pass(
                d_second, norm_ref[2:3, :], hat2, scale2
            )
            low_ref[rows, :] = d_hidden.astype(jnp.bfloat16)
            ngrad_ref[2:3, :] += jnp.sum(d_second * hat2, axis=0, keepdims=True)
            ngrad_ref[3:4, :] += jnp.sum(d_second, axis=0, keepdims=True)
            start_all(results(n))
            return carry

        lax.fori_loop(0, tiles, close, 0)
        for n in range(tiles):
            wait_all(results(n))


def backward_kernel(heads, head_size, half, pack, units, *refs):
    count = len(pack.arrays)
    low_ref, qkv_ref, log_ref = refs[:3]
    raw = refs[3 : 3 + count]
    dqkv_ref, dmix_ref, wout_ref, sems = refs[-4:]
    side = heads // 2 * head_size
    scale = 1.0 / math.sqrt(head_size)
    here = len(pack.pieces) // 2

    @pl.when(pl.program_id(0) == 0)
    def _():
        pairs = []
        for n in range(here):
            pairs += pack.copies(raw, half * here + n, 3 * units, units, wout_ref, n * units)
        copies = copies_on(pairs, sems)
        start_all(copies)
        wait_all(copies)

    low = low_ref[...]
    dmix_ref[...] = dot_right_t(low, wout_ref[...]).astype(jnp.bfloat16)
    low_half = low_lanes(head_size)

    def one_frame(n, carry):
        rows = pl.ds(pl.multiple_of(n * PADDED, 16), PADDED)
        valid = lax.broadcasted_iota(jnp.int32, (1, PADDED), 1) < PLACES

        def part(kind, pair):
            at = kind * side + pair * 2 * head_size
            return slice(at, at + 2 * head_size)

        def begin(pair):
            qm = both_hands(qkv_ref[rows, part(0, pair)] * jnp.bfloat16(scale), low_half)
            gm = both_hands(dmix_ref[rows, part(0, pair)], low_half)
            scores = dot_right_t(qm, qkv_ref[rows, part(1, pair)])
            return qm, gm, scores, dot_right_t(gm, qkv_ref[rows, part(2, pair)])

        def middle(pair, begun):
            qm, gm, scores, d_probs = begun
            head = half * (heads // 2) + 2 * pair
            log_total = jnp.concatenate(
                [log_ref[rows, head : head + 1], log_ref[rows, head + 1 : head + 2]], axis=0
            )
            probs = jnp.exp(jnp.where(valid, scores, LOWEST) - log_total)
            delta = jnp.sum(d_probs * probs, axis=-1, keepdims=True)
            d_scores = (probs * (d_probs - delta)).astype(jnp.bfloat16)
            return qm, gm, probs.astype(jnp.bfloat16), d_scores

        def end(pair, half_done):
            qm, gm, probs_low, d_scores = half_done
            dq = dot_rows(d_scores, qkv_ref[rows, part(1, pair)])
            dq = jnp.where(low_half, dq[:PADDED], dq[PADDED:]) * scale
            dqkv_ref[rows, part(0, pair)] = dq.astype(jnp.bfloat16)
            dqkv_ref[rows, part(1, pair)] = dot_left_t(d_scores, qm).astype(jnp.bfloat16)
            dqkv_ref[rows, part(2, pair)] = dot_left_t(probs_low, gm).astype(jnp.bfloat16)

        staggered(heads // 4, begin, middle, end)
        return carry

    lax.fori_loop(0, low.shape[0] // PADDED, one_frame, 0)


def gradient_kernel(left_ref, right_ref, out_ref):
    out_ref[...] = dot_left_t(left_ref[...], right_ref[...])


def gradients_kernel(left_ref, right_ref, other_ref, *refs):
    out_ref = refs[-1]
    step = pl.program_id(0)

    def put(block):
        if len(refs) > 1:
            block = block + refs[0][...].astype(jnp.float32)
        out_ref[...] = block.astype(out_ref.dtype)

    @pl.when(step < 3)
    def _():
        put(dot_left_t(left_ref[...], right_ref[...]))

    @pl.when(step == 3)
    def _():
        put(other_ref[...])


def input_kernel(pack, units, *refs):
    count = len(pack.arrays)
    x_ref, low_ref, first_ref, last_ref, norm_ref = refs[:5]
    raw = refs[5 : 5 + count]
    grad_ref, ngrad_ref, wqkv_ref, sems = refs[5 + count :]
    side = first_ref.shape[1]

    first = pl.program_id(0) == 0
    copies = copies_on(projection_copies(pack, raw, units, wqkv_ref, range(6)), sems)

    @pl.when(first)
    def _():
        start_all(copies)
        ngrad_ref[...] = jnp.zeros_like(ngrad_ref)

    hat1, scale1 = standardize_rows(x_ref[...].astype(jnp.float32))

    @pl.when(first)
    def _():
        wait_all(copies)

    d_first = dot_rows(first_ref[...], wqkv_ref[:side, :])
    d_first += dot_rows(last_ref[...], wqkv_ref[side:, :])
    total = unpad(low_ref[...].astype(jnp.float32) + norm_backward_pass(d_first, norm_ref[0:1, :], hat1, scale1))
    for n in range(grad_ref.shape[0]):
        grad_ref[n] = total[n * grad_ref.shape[1] : (n + 1) * grad_ref.shape[1]]
    ngrad_ref[0:1, :] += jnp.sum(d_first * hat1, axis=0, keepdims=True)
    ngrad_ref[1:2, :] += jnp.sum(d_first, axis=0, keepdims=True)


def on_device(
    frames_in,
    out_grad,
    w_query,
    w_key,
    w_value,
    w_out,
    w_up,
    w_down,
    norm1_gain,
    norm1_bias,
    norm2_gain,
    norm2_bias,
):
    block_count, resident_rows, width = frames_in.shape
    frames_each = resident_rows // PLACES
    block_rows = frames_each * PADDED
    rows = block_count * block_rows
    two = 2 * block_rows
    head_size = width // HEADS
    units = w_query.shape[1]
    part = w_query.shape[0]
    hidden_units = w_up.shape[1]
    order_a, order_b = orders()
    pieces = lax.axis_size("tp")
    low, full = jnp.bfloat16, jnp.float32
    sds = jax.ShapeDtypeStruct

    near = pl.pallas_call(
        pack_near_kernel,
        name="pack_near",
        out_shape=sds((4 * units, part), low),
        compiler_params=params(),
    )(w_query.T, w_key.T, w_value.T, w_out)
    attention = gather_pack(near)
    norms = gather_columns([norm1_gain, norm1_bias, norm2_gain, norm2_bias]).astype(full)
    feed_here = pl.pallas_call(
        pack_feed_kernel,
        name="pack_feed",
        in_specs=[pl.BlockSpec(memory_space=pltpu.VMEM)] * 2
        + [pl.BlockSpec(memory_space=pl.ANY)],
        out_shape=sds((2 * hidden_units, part), low),
        compiler_params=params(),
    )(w_up, w_down, attention.arrays[1])
    feed = gather_pack(feed_here)

    resident_two = pl.BlockSpec((2, resident_rows, width), lambda i: (i, 0, 0))
    tokens, cotangent, cotangent_t, normed = pl.pallas_call(
        functools.partial(prepare_kernel, frames_each),
        name="prepare",
        out_shape=[
            sds((rows, width), low),
            sds((rows, width), low),
            sds((width, rows), low),
            sds((rows, width), low),
        ],
        compiler_params=params(),
        cost_estimate=cost(9),
    )(frames_in, out_grad, norms)

    qkv, mixed, logs, hidden, second = pl.pallas_call(
        functools.partial(attend_kernel, HEADS, head_size, attention, units),
        name="attend",
        grid=(block_count // 2,),
        in_specs=[rows_of(two, width), rows_of(two, width), whole((8, width))]
        + in_place(attention.arrays),
        out_specs=[
            rows_of(two, 3 * width),
            rows_of(two, width),
            rows_of(two, 128),
            rows_of(two, width),
            rows_of(two, width),
        ],
        out_shape=[
            sds((rows, 3 * width), low),
            sds((rows, width), low),
            sds((rows, 128), full),
            sds((rows, width), full),
            sds((rows, width), low),
        ],
        scratch_shapes=[
            pltpu.VMEM((3 * width, width), low),
            pltpu.VMEM((width, width), low),
            pltpu.SemaphoreType.DMA((64,)),
        ],
        compiler_params=params(),
        cost_estimate=cost(30),
    )(tokens, normed, norms, *attention.arrays)

    second_t = pl.pallas_call(
        turn_kernel,
        name="turn",
        out_shape=sds((width, rows), low),
        compiler_params=params(),
        cost_estimate=cost(5),
    )(second)

    half = pieces // 2
    send_block = pl.BlockSpec(
        (1, 2, width, hidden_units), lambda i: (jnp.minimum(i, half - 1), 0, 0, 0)
    )
    block_out, hidden_low, feed_keep, feed_send, second_terms = pl.pallas_call(
        functools.partial(forward_kernel, block_rows, feed, hidden_units),
        name="feed_forward",
        grid=(pieces,),
        in_specs=in_place((second, cotangent, second_t, cotangent_t, hidden))
        + [whole((8, width))]
        + in_place(feed.arrays),
        out_specs=in_place(("block_out", "hidden_low", "feed_keep"))
        + [send_block, whole((8, width))],
        out_shape=[
            sds(frames_in.shape, low),
            sds((rows, width), low),
            sds((half, 2, width, hidden_units), full),
            sds((half, 2, width, hidden_units), low),
            sds((8, width), full),
        ],
        scratch_shapes=[
            pltpu.VMEM((rows, width), low),
            pltpu.VMEM((rows, width), low),
            pltpu.VMEM((width, rows), low),
            pltpu.VMEM((width, rows), low),
            pltpu.VMEM((rows, width), full),
            pltpu.VMEM((rows, width), full),
            pltpu.VMEM((rows, width), full),
            pltpu.VMEM((rows, hidden_units), low),
            pltpu.VMEM((rows, hidden_units), low),
            pltpu.VMEM((2, hidden_units, width), low),
            pltpu.VMEM((hidden_units, width), low),
            pltpu.VMEM((hidden_units, width), low),
            pltpu.VMEM((width, hidden_units), low),
            pltpu.VMEM((width, hidden_units), low),
            pltpu.VMEM((2, width, hidden_units), full),
            pltpu.VMEM(frames_in.shape, low),
            pltpu.VMEM((rows, width), low),
            pltpu.SemaphoreType.DMA((16,)),
            pltpu.SemaphoreType.DMA((5,)),
            pltpu.SemaphoreType.DMA((1 + block_count,)),
            pltpu.SemaphoreType.DMA((block_count,)),
            pltpu.SemaphoreType.DMA((block_count,)),
        ],
        compiler_params=params(),
        cost_estimate=cost(62),
    )(second, cotangent, second_t, cotangent_t, hidden, norms, *feed.arrays)

    last = order_a[-1]
    steps_a, steps_b = order_a[:-1][::-1], order_b[:-1][::-1]
    feed_got = swap(feed_send, *last)
    side = width // 2
    out_total = pl.pallas_call(
        gradient_kernel,
        name="out_gradient",
        grid=(2,),
        in_specs=[pl.BlockSpec((rows, side), lambda i: (0, i)), whole((rows, width))],
        out_specs=rows_of(side, width),
        out_shape=sds((width, width), full),
        compiler_params=params(),
        cost_estimate=cost(4),
    )(mixed, hidden_low)
    up_held = feed_keep[:, 0] + feed_got[:, 0].astype(full)
    down_held = feed_keep[:, 1] + feed_got[:, 1].astype(full)

    wide = 3 * width // 2

    def attention_back(side, group, begun):
        each = block_count // 4
        base = group * each

        def at(count, columns, column=0):
            return pl.BlockSpec((count, columns), lambda i: (base + i, column))

        begun = () if begun is None else (begun,)
        operands = (hidden_low, qkv, logs) + attention.arrays + begun
        return pl.pallas_call(
            functools.partial(backward_kernel, HEADS, head_size, side, attention, units),
            grid=(each,),
            in_specs=[
                at(two, width),
                at(two, wide, side),
                at(two, 128),
            ]
            + in_place(attention.arrays + begun),
            out_specs=at(two, wide),
            out_shape=sds((rows, wide), low),
            scratch_shapes=[
                pltpu.VMEM((two, width // 2), low),
                pltpu.VMEM((width // 2, width), low),
                pltpu.SemaphoreType.DMA((16,)),
            ],
            input_output_aliases={len(operands) - 1: 0} if begun else {},
            compiler_params=params(),
            cost_estimate=cost(12),
        )(*operands)

    def gradients(left, which, dtype, *came):
        block = pl.BlockSpec((side, width), lambda i: (i, 0))
        return pl.pallas_call(
            gradients_kernel,
            grid=(4,),
            in_specs=[
                pl.BlockSpec((rows, side), lambda i: (0, jnp.minimum(i, 2))),
                whole((rows, width)),
                pl.BlockSpec((side, width), lambda i: (which, 0)),
            ]
            + [block] * len(came),
            out_specs=block,
            out_shape=sds((4 * side, width), dtype),
            compiler_params=params(),
            cost_estimate=cost(8),
        )(left, normed, out_total, *came)

    d_last = attention_back(1, 1, attention_back(1, 0, None))
    near_send = gradients(d_last, 1, low)
    near_got = swap(near_send, *last)
    d_lead = attention_back(0, 1, attention_back(0, 0, None))
    for step_a, step_b in zip(steps_a, steps_b):
        up_held = reduce_step(up_held, step_a, 0, 1)
        down_held = reduce_step(down_held, step_b, 0, 1)
    feed_sum = sum_over_ctx(jnp.concatenate([up_held[0], down_held[0]], axis=0))

    shape = (2, half, units, width)
    lead_total = gradients(d_lead, 0, full, near_got)
    a_held = lead_total[: 2 * side].reshape(shape)
    b_held = lead_total[2 * side :].reshape(shape)

    input_grad, first_terms = pl.pallas_call(
        functools.partial(input_kernel, attention, units),
        name="input_gradient",
        grid=(block_count // 2,),
        in_specs=[
            rows_of(two, width),
            rows_of(two, width),
            rows_of(two, wide),
            rows_of(two, wide),
            whole((8, width)),
        ]
        + in_place(attention.arrays),
        out_specs=[resident_two, whole((8, width))],
        out_shape=[sds(frames_in.shape, full), sds((8, width), full)],
        scratch_shapes=[
            pltpu.VMEM((3 * width, width), low),
            pltpu.SemaphoreType.DMA((64,)),
        ],
        compiler_params=params(),
        cost_estimate=cost(14),
    )(tokens, hidden_low, d_lead, d_last, norms, *attention.arrays)

    for step_a, step_b in zip(steps_a, steps_b):
        a_held = reduce_step(a_held, step_a, 1, 3)
        b_held = reduce_step(b_held, step_b, 1, 3)
    norm_terms = sum_over(
        jnp.where(
            lax.broadcasted_iota(jnp.int32, first_terms.shape, 0) < 2, first_terms, second_terms
        ),
        ("tp", "fsdp", "ctx"),
    )
    norm_terms = lax.dynamic_slice_in_dim(
        norm_terms, lax.axis_index("fsdp") * part, part, 1
    )
    near_sum = sum_over_ctx(
        jnp.concatenate([a_held.reshape(-1, part), b_held.reshape(-1, part)], axis=0),
    )
    return (
        block_out,
        input_grad,
        near_sum[:units].T,
        near_sum[units : 2 * units].T,
        near_sum[2 * units : 3 * units].T,
        near_sum[3 * units :],
        feed_sum[:part],
        feed_sum[part:].T,
        norm_terms[0],
        norm_terms[1],
        norm_terms[2],
        norm_terms[3],
    )


def solution(mesh):
    tokens = P(None, ("fsdp", "ctx", "tp"), None)
    weights = (
        P("fsdp", "tp"),
        P("fsdp", "tp"),
        P("fsdp", "tp"),
        P("tp", "fsdp"),
        P("fsdp", "tp"),
        P("tp", "fsdp"),
        P("fsdp"),
        P("fsdp"),
        P("fsdp"),
        P("fsdp"),
    )
    return jax.shard_map(
        on_device,
        mesh=mesh,
        in_specs=(tokens, tokens) + weights,
        out_specs=(tokens, tokens) + weights,
        check_vma=False,
    )
```

```python
import functools
import math

import jax
import jax.numpy as jnp
from jax import lax
from jax.experimental import pallas as pl
from jax.experimental.pallas import tpu as pltpu
from jax.sharding import PartitionSpec as P


HEADS = 12
PLACES = 196
PADDED = 208

EPSILON = 1e-06
INV_ROOT_TWO = 0.7071067811865476
INV_ROOT_TAU = 0.3989422804014327
LOWEST = -1e30

VMEM_BYTES = 60 * 1024 * 1024


def dot_rows(left, right):
    return lax.dot_general(
        left, right, (((1,), (0,)), ((), ())), preferred_element_type=jnp.float32
    )


def dot_right_t(left, right):
    return lax.dot_general(
        left, right, (((1,), (1,)), ((), ())), preferred_element_type=jnp.float32
    )


def dot_left_t(left, right):
    return lax.dot_general(
        left, right, (((0,), (0,)), ((), ())), preferred_element_type=jnp.float32
    )


def standardize_rows(rows_in):
    center = rows_in - jnp.mean(rows_in, axis=-1, keepdims=True)
    spread = jnp.mean(center * center, axis=-1, keepdims=True)
    reciprocal_spread = lax.rsqrt(spread + EPSILON)
    return (center * reciprocal_spread, reciprocal_spread)


def norm_backward_pass(norm_gradient, gain_vector, centered_rows, reciprocal_spread):
    scaled_result = norm_gradient * gain_vector
    leading_part = jnp.mean(scaled_result, axis=-1, keepdims=True)
    trailing_part = jnp.mean(scaled_result * centered_rows, axis=-1, keepdims=True)
    return reciprocal_spread * (scaled_result - leading_part - centered_rows * trailing_part)


def swap(block, axis, mask):
    count = lax.axis_size(axis)
    return lax.ppermute(block, axis, [(i, i ^ mask) for i in range(count)])


def bits_of(axis):
    return [(axis, 1 << b) for b in reversed(range(lax.axis_size(axis).bit_length() - 1))]


def orders():
    along_f, along_t = bits_of("fsdp"), bits_of("tp")
    first, last = along_t[:-1], along_t[-1:]
    return (along_f + first + last, first + along_f + last)


def piece_masks():
    masks = [0]
    for _, mask in bits_of("tp"):
        masks = [m for m in masks] + [m ^ mask for m in masks]
    return masks


class Pack:
    def __init__(self, arrays, pieces, part):
        self.arrays, self.pieces, self.part = arrays, pieces, part

    def copies(self, refs, piece, first, count, target, row):
        mine = lax.axis_index("fsdp")
        made = []
        for array, start, rows, place, mask in self.pieces[piece]:
            low, high = max(first, place), min(first + count, place + rows)
            if low >= high:
                continue
            source = refs[array].at[pl.ds(start + low - place, high - low), :]
            where = pl.ds(row + low - first, high - low)
            if mask is None:
                made.append((source, target.at[where, :]))
            else:
                column = pl.multiple_of((mine ^ mask) * self.part, 128)
                made.append((source, target.at[where, pl.ds(column, self.part)]))
        return made


def copies_on(pairs, sems, at=0):
    return [
        pltpu.make_async_copy(source, target, sems.at[at + n])
        for n, (source, target) in enumerate(pairs)
    ]


def start_all(copies):
    for copy in copies:
        copy.start()


def wait_all(copies):
    for copy in copies:
        copy.wait()


def gather_pack(block):
    f_count, t_count = lax.axis_size("fsdp"), lax.axis_size("tp")
    rows, part = block.shape
    if f_count == 2 and t_count == 4 and part % 128 == 0:
        half = rows // 2
        beside_f = swap(block, "fsdp", 1)
        beside_t = swap(block, "tp", 2)
        across = (swap(beside_f[:half], "tp", 2), swap(beside_t[half:], "fsdp", 1))
        here = (block, beside_f, beside_t) + across
        there = tuple(swap(array, "tp", 1) for array in here)
        pieces = []
        for base in (0, len(here)):
            pieces.append([(base, 0, rows, 0, 0), (base + 1, 0, rows, 0, 1)])
            pieces.append(
                [
                    (base + 2, 0, rows, 0, 0),
                    (base + 3, 0, half, 0, 1),
                    (base + 4, 0, half, half, 1),
                ]
            )
        return Pack(here + there, pieces, part)
    held, keys = block[None], [(0, 0)]
    for axis, mask in orders()[0]:
        held = jnp.concatenate([held, swap(held, axis, mask)], axis=0)
        keys = keys + [(f ^ mask, t) if axis == "fsdp" else (f, t ^ mask) for f, t in keys]
    place = {key: n for n, key in enumerate(keys)}
    mine = lax.axis_index("fsdp")
    full = []
    for t in piece_masks():
        stacked = jnp.stack([held[place[(f, t)]] for f in range(f_count)])
        parts = [
            lax.dynamic_index_in_dim(stacked, mine ^ f, 0, keepdims=False)
            for f in range(f_count)
        ]
        full.append(jnp.concatenate(parts, axis=1))
    pieces = [[(p, 0, rows, 0, None)] for p in range(t_count)]
    return Pack(tuple(full), pieces, part)


def gather_columns(vectors):
    held, masks = [jnp.concatenate(vectors)], [0]
    for axis, mask in bits_of("fsdp"):
        got = swap(jnp.concatenate(held), axis, mask)
        held = held + jnp.split(got, len(held))
        masks = masks + [m ^ mask for m in masks]
    mine = lax.axis_index("fsdp")
    count = len(held)
    parts = [held[masks.index(m)].reshape(len(vectors), -1) for m in range(count)]
    if count == 2:
        first = mine == 0
        parts = [jnp.where(first, parts[0], parts[1]), jnp.where(first, parts[1], parts[0])]
    else:
        stacked = jnp.stack(parts)
        parts = [
            lax.dynamic_index_in_dim(stacked, mine ^ m, 0, keepdims=False) for m in range(count)
        ]
    return jnp.pad(jnp.concatenate(parts, axis=1), ((0, 8 - len(vectors)), (0, 0)))


def reduce_step(held, step, piece_axis, part_axis):
    axis, mask = step
    if axis == "tp":
        half = held.shape[piece_axis] // 2
        keep = lax.slice_in_dim(held, 0, half, axis=piece_axis)
        sent = lax.slice_in_dim(held, half, 2 * half, axis=piece_axis)
    else:
        part = held.shape[part_axis] // 2
        bit = jnp.where((lax.axis_index("fsdp") & mask) != 0, 1, 0)
        keep = lax.dynamic_slice_in_dim(held, bit * part, part, part_axis)
        sent = lax.dynamic_slice_in_dim(held, (1 - bit) * part, part, part_axis)
    return keep + swap(sent.astype(jnp.bfloat16), axis, mask).astype(jnp.float32)


def sum_over_ctx(block):
    count = lax.axis_size("ctx")
    bit = lax.axis_index("ctx") & 1
    rows = block.shape[0] // 2
    sent = lax.dynamic_slice_in_dim(block, (1 - bit) * rows, rows, 0)
    got = swap(sent.astype(jnp.bfloat16), "ctx", 1)
    held = lax.dynamic_slice_in_dim(block, bit * rows, rows, 0) + got.astype(jnp.float32)
    mask = 2
    while mask < count:
        got = swap(held.astype(jnp.bfloat16), "ctx", mask)
        held = held + got.astype(jnp.float32)
        mask *= 2
    other = swap(held.astype(jnp.bfloat16), "ctx", 1).astype(jnp.float32)
    return jnp.where(
        bit == 0,
        jnp.concatenate([held, other], axis=0),
        jnp.concatenate([other, held], axis=0),
    )


def sum_over(block, axes):
    for axis in axes:
        for _, mask in reversed(bits_of(axis)):
            block = block + swap(block, axis, mask)
    return block


def params():
    return pltpu.CompilerParams(vmem_limit_bytes=VMEM_BYTES)


def cost(micros):
    return pl.CostEstimate(flops=int(micros * 1.1e9), bytes_accessed=0, transcendentals=0)


def whole(shape):
    return pl.BlockSpec(shape, lambda i: (0,) * len(shape), pipeline_mode=pl.Buffered(1))


def rows_of(count, width, column=0):
    return pl.BlockSpec((count, width), lambda i: (i, column))


def in_place(arrays):
    return [pl.BlockSpec(memory_space=pl.ANY)] * len(arrays)


def prepare_kernel(count, x_ref, g_ref, norm_ref, xo_ref, go_ref, got_ref, xn_ref):
    blank = jnp.zeros((PADDED - PLACES, x_ref.shape[2]), jnp.float32)
    block_rows = count * PADDED

    def padded(block):
        parts = []
        for n in range(count):
            parts += [block[n * PLACES : (n + 1) * PLACES], blank]
        return jnp.concatenate(parts, axis=0)

    def one_block(n, carry):
        rows = pl.ds(pl.multiple_of(n * block_rows, 16), block_rows)
        tokens = padded(x_ref[n].astype(jnp.float32))
        xo_ref[rows, :] = tokens.astype(jnp.bfloat16)
        hat, _ = standardize_rows(tokens)
        xn_ref[rows, :] = (hat * norm_ref[0:1, :] + norm_ref[1:2, :]).astype(jnp.bfloat16)
        go_ref[rows, :] = padded(g_ref[n].astype(jnp.float32)).astype(jnp.bfloat16)
        return carry

    lax.fori_loop(0, x_ref.shape[0], one_block, 0)
    turn(go_ref, got_ref)


def turn(source, target):
    def one(n, carry):
        part = pl.ds(pl.multiple_of(n * 128, 128), 128)
        target[:, part] = source[part, :].T
        return carry

    lax.fori_loop(0, source.shape[0] // 128, one, 0)


def turn_kernel(source_ref, target_ref):
    turn(source_ref, target_ref)


def pack_near_kernel(q_ref, k_ref, v_ref, o_ref, out_ref):
    units = q_ref.shape[0]
    for n, ref in enumerate((q_ref, k_ref, v_ref, o_ref)):
        out_ref[n * units : (n + 1) * units, :] = ref[...]


def pack_feed_kernel(up_ref, down_ref, gate_ref, out_ref):
    units = up_ref.shape[1]
    out_ref[:units, :] = up_ref[...].T
    out_ref[units:, :] = down_ref[...]


def unpad(block):
    count = block.shape[0] // PADDED
    return jnp.concatenate(
        [block[n * PADDED : n * PADDED + PLACES] for n in range(count)], axis=0
    )


def low_lanes(head_size):
    lane = lax.broadcasted_iota(jnp.int32, (1, 2 * head_size), 1)
    return lane < head_size


def staggered(count, begin, middle, end):
    begun, half_done = {0: begin(0)}, {}
    for n in range(count + 1):
        if n + 1 < count:
            begun[n + 1] = begin(n + 1)
        if n < count:
            half_done[n] = middle(n, begun.pop(n))
        if n > 0:
            end(n - 1, half_done.pop(n - 1))


def both_hands(block, low_half):
    blank = jnp.zeros_like(block)
    return jnp.concatenate(
        [jnp.where(low_half, block, blank), jnp.where(low_half, blank, block)], axis=0
    )


def projection_copies(pack, refs, units, target, groups):
    pieces = len(pack.pieces)
    side = pieces // 2 * units
    made = []
    for group in groups:
        half, kind = divmod(group, 3)
        for n in range(pieces // 2):
            row = group * side + n * units
            made += pack.copies(
                refs, half * pieces // 2 + n, kind * units, units, target, row
            )
    return made


def attend_kernel(heads, head_size, pack, units, *refs):
    count = len(pack.arrays)
    x_ref, xn_ref, norm_ref = refs[:3]
    raw = refs[3 : 3 + count]
    qkv_ref, mixed_ref, log_ref, hidden_ref, sn_ref = refs[3 + count : 8 + count]
    wqkv_ref, wout_ref, sems = refs[8 + count :]
    width = heads * head_size
    side = width // 2

    first = pl.program_id(0) == 0
    batches, used = [], 0
    for n in range(3):
        pairs = projection_copies(pack, raw, units, wqkv_ref, (2 * n, 2 * n + 1))
        batches.append(copies_on(pairs, sems, used))
        used += len(pairs)
    pairs = []
    for p in range(len(pack.pieces)):
        pairs += pack.copies(raw, p, 3 * units, units, wout_ref, p * units)
    batches.append(copies_on(pairs, sems, used))

    @pl.when(first)
    def _():
        for batch in batches:
            start_all(batch)

    normed = xn_ref[...]

    def project(n, carry):
        for k in range(3):

            @pl.when(first & (n == k))
            def _(k=k):
                wait_all(batches[k])

        cut = pl.ds(pl.multiple_of(n * width, 128), width)
        qkv_ref[:, cut] = dot_right_t(normed, wqkv_ref[cut, :]).astype(jnp.bfloat16)
        return carry

    lax.fori_loop(0, 3, project, 0)
    low_half = low_lanes(head_size)
    scale = 1.0 / math.sqrt(head_size)

    def one_frame(n, carry):
        rows = pl.ds(pl.multiple_of(n * PADDED, 16), PADDED)
        valid = lax.broadcasted_iota(jnp.int32, (1, PADDED), 1) < PLACES

        def begin(pair):
            half, place = divmod(pair, heads // 4)
            at = 3 * half * side + place * 2 * head_size
            q2 = qkv_ref[rows, at : at + 2 * head_size] * jnp.bfloat16(scale)
            k2 = qkv_ref[rows, side + at : side + at + 2 * head_size]
            return dot_right_t(both_hands(q2, low_half), k2)

        def middle(pair, scores):
            scores = jnp.where(valid, scores, LOWEST)
            top = jnp.max(scores, axis=-1, keepdims=True)
            powers = jnp.exp(scores - top)
            total = jnp.sum(powers, axis=-1, keepdims=True)
            logs = top + jnp.log(total)
            log_ref[rows, 2 * pair : 2 * pair + 1] = logs[:PADDED]
            log_ref[rows, 2 * pair + 1 : 2 * pair + 2] = logs[PADDED:]
            return (powers * (1.0 / total)).astype(jnp.bfloat16)

        def end(pair, probs):
            half, place = divmod(pair, heads // 4)
            at = (3 * half + 2) * side + place * 2 * head_size
            outs = dot_rows(probs, qkv_ref[rows, at : at + 2 * head_size])
            mixed_ref[rows, 2 * pair * head_size : 2 * (pair + 1) * head_size] = jnp.where(
                low_half, outs[:PADDED], outs[PADDED:]
            ).astype(jnp.bfloat16)

        staggered(heads // 2, begin, middle, end)
        return carry

    lax.fori_loop(0, normed.shape[0] // PADDED, one_frame, 0)

    @pl.when(first)
    def _():
        wait_all(batches[3])

    hidden = x_ref[...].astype(jnp.float32) + dot_rows(mixed_ref[...], wout_ref[...])
    hidden_ref[...] = hidden
    hat2, _ = standardize_rows(hidden)
    sn_ref[...] = (hat2 * norm_ref[2:3, :] + norm_ref[3:4, :]).astype(jnp.bfloat16)


def forward_kernel(tile, pack, units, *refs):
    count = len(pack.arrays)
    arrays, norm_ref = refs[:5], refs[5]
    raw = refs[6 : 6 + count]
    out_any, low_any, keep_any, send_ref, ngrad_ref = refs[6 + count : 11 + count]
    held = refs[11 + count : 15 + count]
    sn_ref, cot_ref, turned_ref, hidden_ref = held
    (
        y_ref, dh_ref, by_ref, next_ref, wup_ref, wdown_ref, wupt_ref, wdownt_ref,
        keep_ref, out_ref, low_ref, sems, held_sems, keep_sems, out_sems, low_sems,
    ) = refs[15 + count :]
    step, steps = pl.program_id(0), len(pack.pieces)
    tiles = sn_ref.shape[0] // tile
    chunk = sn_ref.shape[1] // tiles
    wide = 2 * tile
    order = [(n + steps // 2) % steps for n in range(steps)]
    targets = (sn_ref, cot_ref, turned_ref.at[0], turned_ref.at[1], hidden_ref)
    late = copies_on(zip(arrays, targets), held_sems)

    def copies_of(n):
        pairs = pack.copies(raw, order[n], 0, units, next_ref.at[0], 0)
        pairs += pack.copies(raw, order[n], units, units, next_ref.at[1], 0)
        return copies_on(pairs, sems)

    @pl.when(step == 0)
    def _():
        start_all(copies_of(0) + late)
        y_ref[...] = jnp.zeros_like(y_ref)
        dh_ref[...] = jnp.zeros_like(dh_ref)

    def settle(n, size):
        rows = pl.ds(pl.multiple_of(n * size, 128), size)
        for place, plain, turned in ((0, wup_ref, wupt_ref), (1, wdown_ref, wdownt_ref)):
            block = next_ref[place, rows, :]
            plain[rows, :] = block
            turned[:, rows] = block.T

    def settle_all():
        def one(n, carry):
            settle(n, units // 2)
            return carry

        lax.fori_loop(0, 2, one, 0)

    @pl.when(step == 0)
    def _():
        wait_all(copies_of(0))
        settle_all()
        start_all(copies_of(1))
        wait_all(late[:2])

    def one_tile(n, carry):
        rows = pl.ds(pl.multiple_of(n * wide, 16), wide)
        inner = dot_rows(sn_ref[rows, :], wupt_ref[...])
        d_active = dot_rows(cot_ref[rows, :], wdownt_ref[...])
        share = 0.5 * (1.0 + lax.erf(inner * INV_ROOT_TWO))
        active = (inner * share).astype(jnp.bfloat16)
        slope = share + inner * (jnp.exp(-0.5 * inner * inner) * INV_ROOT_TAU)
        d_inner = (d_active * slope).astype(jnp.bfloat16)
        by_ref[1, rows, :] = active
        by_ref[0, rows, :] = d_inner
        y_ref[rows, :] += dot_rows(active, wdown_ref[...])
        dh_ref[rows, :] += dot_rows(d_inner, wup_ref[...])
        return carry

    lax.fori_loop(0, tiles // 2, one_tile, 0)

    @pl.when(step == 0)
    def _():
        wait_all(late[2:4])

    def weight_gradient(n, rows):
        keep_ref[n, rows, :] = dot_rows(turned_ref[n, rows, :], by_ref[n])

    def whole_keep(p):
        return pltpu.make_async_copy(
            keep_ref, keep_any.at[p - steps // 2], keep_sems.at[0]
        )

    for p in range(steps // 2 + 1, steps):

        @pl.when(step == p)
        def _(p=p):
            whole_keep(p - 1).wait()

    for p in range(1, steps):

        @pl.when(step == p - 1)
        def _(p=p):
            wait_all(copies_of(p))

    @pl.when(step < steps - 1)
    def _():
        def one(n, carry):
            weight_gradient(n, slice(None))
            settle(n, units // 2)
            return carry

        lax.fori_loop(0, 2, one, 0)

    @pl.when(step < steps // 2)
    def _():
        send_ref[0] = keep_ref[...].astype(jnp.bfloat16)

    for p in range(steps // 2, steps - 1):

        @pl.when(step == p)
        def _(p=p):
            whole_keep(p).start()

    for p in range(2, steps):

        @pl.when(step == p - 2)
        def _(p=p):
            start_all(copies_of(p))

    @pl.when(step == steps - 1)
    def _():
        ngrad_ref[...] = jnp.zeros_like(ngrad_ref)
        wait_all(late[4:])

        def results(n):
            rows = pl.ds(pl.multiple_of(n * tile, 16), tile)
            part = pl.ds(pl.multiple_of(n * chunk, 16), chunk)
            return [
                pltpu.make_async_copy(out_ref.at[n], out_any.at[n], out_sems.at[n]),
                pltpu.make_async_copy(low_ref.at[rows, :], low_any.at[rows, :], low_sems.at[n]),
                pltpu.make_async_copy(
                    keep_ref.at[:, part, :],
                    keep_any.at[steps // 2 - 1, :, part, :],
                    keep_sems.at[1 + n],
                ),
            ]

        def close(n, carry):
            for m in range(2):
                weight_gradient(m, pl.ds(pl.multiple_of(n * chunk, 16), chunk))
            rows = pl.ds(pl.multiple_of(n * tile, 16), tile)
            hidden = hidden_ref[rows, :]
            out_ref[n] = unpad(hidden + y_ref[rows, :]).astype(jnp.bfloat16)
            hat2, scale2 = standardize_rows(hidden)
            d_second = dh_ref[rows, :]
            d_hidden = cot_ref[rows, :].astype(jnp.float32) + norm_backward_pass(
                d_second, norm_ref[2:3, :], hat2, scale2
            )
            low_ref[rows, :] = d_hidden.astype(jnp.bfloat16)
            ngrad_ref[2:3, :] += jnp.sum(d_second * hat2, axis=0, keepdims=True)
            ngrad_ref[3:4, :] += jnp.sum(d_second, axis=0, keepdims=True)
            start_all(results(n))
            return carry

        lax.fori_loop(0, tiles, close, 0)
        for n in range(tiles):
            wait_all(results(n))


def backward_kernel(heads, head_size, half, pack, units, *refs):
    count = len(pack.arrays)
    low_ref, qkv_ref, log_ref = refs[:3]
    raw = refs[3 : 3 + count]
    dqkv_ref, dmix_ref, wout_ref, sems = refs[-4:]
    side = heads // 2 * head_size
    scale = 1.0 / math.sqrt(head_size)
    here = len(pack.pieces) // 2

    @pl.when(pl.program_id(0) == 0)
    def _():
        pairs = []
        for n in range(here):
            pairs += pack.copies(raw, half * here + n, 3 * units, units, wout_ref, n * units)
        copies = copies_on(pairs, sems)
        start_all(copies)
        wait_all(copies)

    low = low_ref[...]
    dmix_ref[...] = dot_right_t(low, wout_ref[...]).astype(jnp.bfloat16)
    low_half = low_lanes(head_size)

    def one_frame(n, carry):
        rows = pl.ds(pl.multiple_of(n * PADDED, 16), PADDED)
        valid = lax.broadcasted_iota(jnp.int32, (1, PADDED), 1) < PLACES

        def part(kind, pair):
            at = kind * side + pair * 2 * head_size
            return slice(at, at + 2 * head_size)

        def begin(pair):
            qm = both_hands(qkv_ref[rows, part(0, pair)] * jnp.bfloat16(scale), low_half)
            gm = both_hands(dmix_ref[rows, part(0, pair)], low_half)
            scores = dot_right_t(qm, qkv_ref[rows, part(1, pair)])
            return qm, gm, scores, dot_right_t(gm, qkv_ref[rows, part(2, pair)])

        def middle(pair, begun):
            qm, gm, scores, d_probs = begun
            head = half * (heads // 2) + 2 * pair
            log_total = jnp.concatenate(
                [log_ref[rows, head : head + 1], log_ref[rows, head + 1 : head + 2]], axis=0
            )
            probs = jnp.exp(jnp.where(valid, scores, LOWEST) - log_total)
            delta = jnp.sum(d_probs * probs, axis=-1, keepdims=True)
            d_scores = (probs * (d_probs - delta)).astype(jnp.bfloat16)
            return qm, gm, probs.astype(jnp.bfloat16), d_scores

        def end(pair, half_done):
            qm, gm, probs_low, d_scores = half_done
            dq = dot_rows(d_scores, qkv_ref[rows, part(1, pair)])
            dq = jnp.where(low_half, dq[:PADDED], dq[PADDED:]) * scale
            dqkv_ref[rows, part(0, pair)] = dq.astype(jnp.bfloat16)
            dqkv_ref[rows, part(1, pair)] = dot_left_t(d_scores, qm).astype(jnp.bfloat16)
            dqkv_ref[rows, part(2, pair)] = dot_left_t(probs_low, gm).astype(jnp.bfloat16)

        staggered(heads // 4, begin, middle, end)
        return carry

    lax.fori_loop(0, low.shape[0] // PADDED, one_frame, 0)


def gradient_kernel(left_ref, right_ref, out_ref):
    out_ref[...] = dot_left_t(left_ref[...], right_ref[...])


def gradients_kernel(left_ref, right_ref, other_ref, *refs):
    out_ref = refs[-1]
    step = pl.program_id(0)

    def put(block):
        if len(refs) > 1:
            block = block + refs[0][...].astype(jnp.float32)
        out_ref[...] = block.astype(out_ref.dtype)

    @pl.when(step < 3)
    def _():
        put(dot_left_t(left_ref[...], right_ref[...]))

    @pl.when(step == 3)
    def _():
        put(other_ref[...])


def input_kernel(pack, units, *refs):
    count = len(pack.arrays)
    x_ref, low_ref, first_ref, last_ref, norm_ref = refs[:5]
    raw = refs[5 : 5 + count]
    grad_ref, ngrad_ref, wqkv_ref, sems = refs[5 + count :]
    side = first_ref.shape[1]

    first = pl.program_id(0) == 0
    copies = copies_on(projection_copies(pack, raw, units, wqkv_ref, range(6)), sems)

    @pl.when(first)
    def _():
        start_all(copies)
        ngrad_ref[...] = jnp.zeros_like(ngrad_ref)

    hat1, scale1 = standardize_rows(x_ref[...].astype(jnp.float32))

    @pl.when(first)
    def _():
        wait_all(copies)

    d_first = dot_rows(first_ref[...], wqkv_ref[:side, :])
    d_first += dot_rows(last_ref[...], wqkv_ref[side:, :])
    total = unpad(low_ref[...].astype(jnp.float32) + norm_backward_pass(d_first, norm_ref[0:1, :], hat1, scale1))
    for n in range(grad_ref.shape[0]):
        grad_ref[n] = total[n * grad_ref.shape[1] : (n + 1) * grad_ref.shape[1]]
    ngrad_ref[0:1, :] += jnp.sum(d_first * hat1, axis=0, keepdims=True)
    ngrad_ref[1:2, :] += jnp.sum(d_first, axis=0, keepdims=True)


def on_device(
    frames_in,
    out_grad,
    w_query,
    w_key,
    w_value,
    w_out,
    w_up,
    w_down,
    norm1_gain,
    norm1_bias,
    norm2_gain,
    norm2_bias,
):
    block_count, resident_rows, width = frames_in.shape
    frames_each = resident_rows // PLACES
    block_rows = frames_each * PADDED
    rows = block_count * block_rows
    two = 2 * block_rows
    head_size = width // HEADS
    units = w_query.shape[1]
    part = w_query.shape[0]
    hidden_units = w_up.shape[1]
    order_a, order_b = orders()
    pieces = lax.axis_size("tp")
    low, full = jnp.bfloat16, jnp.float32
    sds = jax.ShapeDtypeStruct

    near = pl.pallas_call(
        pack_near_kernel,
        out_shape=sds((4 * units, part), low),
        compiler_params=params(),
    )(w_query.T, w_key.T, w_value.T, w_out)
    attention = gather_pack(near)
    norms = gather_columns([norm1_gain, norm1_bias, norm2_gain, norm2_bias]).astype(full)
    feed_here = pl.pallas_call(
        pack_feed_kernel,
        in_specs=[pl.BlockSpec(memory_space=pltpu.VMEM)] * 2
        + [pl.BlockSpec(memory_space=pl.ANY)],
        out_shape=sds((2 * hidden_units, part), low),
        compiler_params=params(),
    )(w_up, w_down, attention.arrays[1])
    feed = gather_pack(feed_here)

    resident_two = pl.BlockSpec((2, resident_rows, width), lambda i: (i, 0, 0))
    tokens, cotangent, cotangent_t, normed = pl.pallas_call(
        functools.partial(prepare_kernel, frames_each),
        out_shape=[
            sds((rows, width), low),
            sds((rows, width), low),
            sds((width, rows), low),
            sds((rows, width), low),
        ],
        compiler_params=params(),
        cost_estimate=cost(9),
    )(frames_in, out_grad, norms)

    qkv, mixed, logs, hidden, second = pl.pallas_call(
        functools.partial(attend_kernel, HEADS, head_size, attention, units),
        grid=(block_count // 2,),
        in_specs=[rows_of(two, width), rows_of(two, width), whole((8, width))]
        + in_place(attention.arrays),
        out_specs=[
            rows_of(two, 3 * width),
            rows_of(two, width),
            rows_of(two, 128),
            rows_of(two, width),
            rows_of(two, width),
        ],
        out_shape=[
            sds((rows, 3 * width), low),
            sds((rows, width), low),
            sds((rows, 128), full),
            sds((rows, width), full),
            sds((rows, width), low),
        ],
        scratch_shapes=[
            pltpu.VMEM((3 * width, width), low),
            pltpu.VMEM((width, width), low),
            pltpu.SemaphoreType.DMA((64,)),
        ],
        compiler_params=params(),
        cost_estimate=cost(30),
    )(tokens, normed, norms, *attention.arrays)

    second_t = pl.pallas_call(
        turn_kernel,
        out_shape=sds((width, rows), low),
        compiler_params=params(),
        cost_estimate=cost(5),
    )(second)

    half = pieces // 2
    send_block = pl.BlockSpec(
        (1, 2, width, hidden_units), lambda i: (jnp.minimum(i, half - 1), 0, 0, 0)
    )
    block_out, hidden_low, feed_keep, feed_send, second_terms = pl.pallas_call(
        functools.partial(forward_kernel, block_rows, feed, hidden_units),
        grid=(pieces,),
        in_specs=in_place((second, cotangent, second_t, cotangent_t, hidden))
        + [whole((8, width))]
        + in_place(feed.arrays),
        out_specs=in_place((0, 0, 0))
        + [send_block, whole((8, width))],
        out_shape=[
            sds(frames_in.shape, low),
            sds((rows, width), low),
            sds((half, 2, width, hidden_units), full),
            sds((half, 2, width, hidden_units), low),
            sds((8, width), full),
        ],
        scratch_shapes=[
            pltpu.VMEM((rows, width), low),
            pltpu.VMEM((rows, width), low),
            pltpu.VMEM((2, width, rows), low),
            pltpu.VMEM((rows, width), full),
            pltpu.VMEM((rows, width), full),
            pltpu.VMEM((rows, width), full),
            pltpu.VMEM((2, rows, hidden_units), low),
            pltpu.VMEM((2, hidden_units, width), low),
            pltpu.VMEM((hidden_units, width), low),
            pltpu.VMEM((hidden_units, width), low),
            pltpu.VMEM((width, hidden_units), low),
            pltpu.VMEM((width, hidden_units), low),
            pltpu.VMEM((2, width, hidden_units), full),
            pltpu.VMEM(frames_in.shape, low),
            pltpu.VMEM((rows, width), low),
            pltpu.SemaphoreType.DMA((16,)),
            pltpu.SemaphoreType.DMA((5,)),
            pltpu.SemaphoreType.DMA((1 + block_count,)),
            pltpu.SemaphoreType.DMA((block_count,)),
            pltpu.SemaphoreType.DMA((block_count,)),
        ],
        compiler_params=params(),
        cost_estimate=cost(62),
    )(second, cotangent, second_t, cotangent_t, hidden, norms, *feed.arrays)

    last = order_a[-1]
    steps_a, steps_b = order_a[:-1][::-1], order_b[:-1][::-1]
    feed_got = swap(feed_send, *last)
    side = width // 2
    out_total = pl.pallas_call(
        gradient_kernel,
        grid=(2,),
        in_specs=[pl.BlockSpec((rows, side), lambda i: (0, i)), whole((rows, width))],
        out_specs=rows_of(side, width),
        out_shape=sds((width, width), full),
        compiler_params=params(),
        cost_estimate=cost(4),
    )(mixed, hidden_low)
    up_held = feed_keep[:, 0] + feed_got[:, 0].astype(full)
    down_held = feed_keep[:, 1] + feed_got[:, 1].astype(full)

    wide = 3 * width // 2

    def attention_back(side):
        each = block_count // 2

        def at(count, columns, column=0):
            return pl.BlockSpec((count, columns), lambda i: (i, column))

        operands = (hidden_low, qkv, logs) + attention.arrays
        return pl.pallas_call(
            functools.partial(backward_kernel, HEADS, head_size, side, attention, units),
            grid=(each,),
            in_specs=[
                at(two, width),
                at(two, wide, side),
                at(two, 128),
            ]
            + in_place(attention.arrays),
            out_specs=at(two, wide),
            out_shape=sds((rows, wide), low),
            scratch_shapes=[
                pltpu.VMEM((two, width // 2), low),
                pltpu.VMEM((width // 2, width), low),
                pltpu.SemaphoreType.DMA((16,)),
            ],
            compiler_params=params(),
            cost_estimate=cost(24),
        )(*operands)

    def gradients(left, which, dtype, *came):
        block = pl.BlockSpec((side, width), lambda i: (i, 0))
        return pl.pallas_call(
            gradients_kernel,
            grid=(4,),
            in_specs=[
                pl.BlockSpec((rows, side), lambda i: (0, jnp.minimum(i, 2))),
                whole((rows, width)),
                pl.BlockSpec((side, width), lambda i: (which, 0)),
            ]
            + [block] * len(came),
            out_specs=block,
            out_shape=sds((4 * side, width), dtype),
            compiler_params=params(),
            cost_estimate=cost(8),
        )(left, normed, out_total, *came)

    d_last = attention_back(1)
    near_send = gradients(d_last, 1, low)
    near_got = swap(near_send, *last)
    d_lead = attention_back(0)
    for step_a, step_b in zip(steps_a, steps_b):
        up_held = reduce_step(up_held, step_a, 0, 1)
        down_held = reduce_step(down_held, step_b, 0, 1)
    feed_sum = sum_over_ctx(jnp.concatenate([up_held[0], down_held[0]], axis=0))

    shape = (2, half, units, width)
    lead_total = gradients(d_lead, 0, full, near_got)
    a_held = lead_total[: 2 * side].reshape(shape)
    b_held = lead_total[2 * side :].reshape(shape)

    input_grad, first_terms = pl.pallas_call(
        functools.partial(input_kernel, attention, units),
        grid=(block_count // 2,),
        in_specs=[
            rows_of(two, width),
            rows_of(two, width),
            rows_of(two, wide),
            rows_of(two, wide),
            whole((8, width)),
        ]
        + in_place(attention.arrays),
        out_specs=[resident_two, whole((8, width))],
        out_shape=[sds(frames_in.shape, full), sds((8, width), full)],
        scratch_shapes=[
            pltpu.VMEM((3 * width, width), low),
            pltpu.SemaphoreType.DMA((64,)),
        ],
        compiler_params=params(),
        cost_estimate=cost(14),
    )(tokens, hidden_low, d_lead, d_last, norms, *attention.arrays)

    for step_a, step_b in zip(steps_a, steps_b):
        a_held = reduce_step(a_held, step_a, 1, 3)
        b_held = reduce_step(b_held, step_b, 1, 3)
    norm_terms = sum_over(
        jnp.where(
            lax.broadcasted_iota(jnp.int32, first_terms.shape, 0) < 2, first_terms, second_terms
        ),
        ("tp", "fsdp", "ctx"),
    )
    norm_terms = lax.dynamic_slice_in_dim(
        norm_terms, lax.axis_index("fsdp") * part, part, 1
    )
    near_sum = sum_over_ctx(
        jnp.concatenate([a_held.reshape(-1, part), b_held.reshape(-1, part)], axis=0),
    )
    return (
        block_out,
        input_grad,
        near_sum[:units].T,
        near_sum[units : 2 * units].T,
        near_sum[2 * units : 3 * units].T,
        near_sum[3 * units :],
        feed_sum[:part],
        feed_sum[part:].T,
        norm_terms[0],
        norm_terms[1],
        norm_terms[2],
        norm_terms[3],
    )


def solution(mesh):
    tokens = P(None, ("fsdp", "ctx", "tp"), None)
    weights = (
        P("fsdp", "tp"),
        P("fsdp", "tp"),
        P("fsdp", "tp"),
        P("tp", "fsdp"),
        P("fsdp", "tp"),
        P("tp", "fsdp"),
        P("fsdp"),
        P("fsdp"),
        P("fsdp"),
        P("fsdp"),
    )
    return jax.shard_map(
        on_device,
        mesh=mesh,
        in_specs=(tokens, tokens) + weights,
        out_specs=(tokens, tokens) + weights,
        check_vma=False,
    )
```
